1024 devices in a mesh: lat: 16 (over y_hi, x), lon: 64 (over y_lo, z, core).
Axes of the slice: x: 4, y: 8 (y_hi: 4, y_lo: 2; y = y_hi * 2 + y_lo), z: 16, core: 2. Of those that a mesh axis runs over, the one named last changes fastest.
Arguments:
- ens_control: bfloat16 [64, 3, 4, 64, 8192], P(None, None, None, 'lat', 'lon'), may hold values from -6 to 6
- perturbations: bfloat16 [64, 3, 4, 64, 8192], P(None, None, None, 'lat', 'lon'), may hold values from -6 to 6
- zonal_control: float32 [3, 4, 64], P(None, None, 'lat'), may hold values from -6 to 6
- spread: float32 [3, 4, 64, 8192], P(None, None, 'lat', 'lon'), may hold values from 0.3 to 3
- currents: float32 [2, 4, 64, 8192], P(None, None, 'lat', 'lon'), may hold values from -0.4 to 0.4
- sea_mask: int32 [64, 8192], P('lat', 'lon'), may hold values 0 or 1
- observed: float32 [2, 3, 4, 64, 8192], P(None, None, None, 'lat', 'lon'), may hold values from -6 to 6
- loc_reach: int32 [8], replicated, may hold values from 0 to 2, as said below
Outputs:
- ens_grad: float32 [64, 3, 4, 64, 8192], P(None, None, None, 'lat', 'lon')
- zonal_grad: float32 [3, 4, 64], P(None, None, 'lat')
The draws below stay inside these ranges and needn't reach their ends.
Inputs may be any that keep to these rules, and one draw needn't show every extreme that they name: `loc_reach`: some block has reach 2 and some block has reach 0.
All inputs are finite; a program needn't handle non-finite values. No bound on the sum of `sea_mask` on one device may be relied on, other than what follows from the above.
Results may differ from the reference program's by a relative error of at most 0.0029.
Values may be sent and summed in bfloat16 or wider, within the bound.
No kernel may reach another device: no remote copies, remote signals or barrier semaphores. Data moves between devices by JAX's collectives and lax.ppermute only.
A program may use at most 32 MiB of HBM per device.

```python
import math
import jax
import jax.numpy as jnp
from jax import lax

MEMB = 64
NBLK = 8
LEV = 4
CLAT = 4
BANDS = 16
NLAT = 64
NLON = 8192
REACH = 2


def draw_loc_reach(key, part):
    base_key = jax.random.fold_in(key, 11)
    level_key, ranking_key = jax.random.split(base_key)
    levels = jax.random.randint(level_key, (NBLK,), 0, REACH + 1)
    ranking = jax.random.permutation(ranking_key, NBLK)
    levels = levels.at[ranking[0]].set(REACH).at[ranking[1]].set(0)
    return levels.astype(jnp.int32)


def place_ends(entries, own_key, least, high):
    spot = [jax.random.randint(jax.random.fold_in(own_key, axis), (), 0, length) for axis, length in enumerate(entries.shape)]
    longest = entries.shape.index(max(entries.shape))
    beside = spot[:longest] + [(spot[longest] + 1) % entries.shape[longest]] + spot[longest + 1:]
    return entries.at[tuple(spot)].set(least).at[tuple(beside)].set(high)


def shard_levels(key, extent, cuts, low, largest):
    loudness = 1.0
    for dim, parts in cuts:
        draws = jax.random.uniform(jax.random.fold_in(jax.random.fold_in(key, 6), dim), (parts,), jnp.float32, low / len(cuts), largest / len(cuts))
        loudness = loudness * jnp.repeat(jnp.exp(draws), extent[dim] // parts).reshape((-1,) + (1,) * (len(extent) - 1 - dim))
    return loudness


def gaussian(own_key, shape, width, reach, cuts=(), held_as=jnp.bfloat16):
    result = width * jax.random.normal(own_key, shape, jnp.float32)
    if cuts:
        result = result * shard_levels(own_key, shape, cuts, -0.22, 0.18)
    return jnp.clip(result, -reach, reach).astype(held_as)


def setup_inputs(seed: int = 0) -> dict:
    keys = jax.random.split(jax.random.key(seed), 9)
    return {
        "ens_control": gaussian(keys[0], (MEMB, 3, LEV, NLAT, NLON), 1.0, 6.0, ((3, 16), (4, 64))),
        "perturbations": gaussian(keys[1], (MEMB, 3, LEV, NLAT, NLON), 1.0, 6.0, ((3, 16), (4, 64))),
        "zonal_control": gaussian(keys[2], (3, LEV, NLAT), 1.0, 6.0, ((2, 16),), jnp.float32),
        "spread": jnp.clip(jnp.exp(math.log(3.0) - 2.3025851 * jax.random.uniform(keys[3], (3, LEV, NLAT, NLON), jnp.float32) ** shard_levels(keys[3], (3, LEV, NLAT, NLON), ((2, 16), (3, 64)), -0.2, 0.2)), 0.3, 3.0),
        "currents": jnp.clip(jax.random.uniform(keys[4], (2, LEV, NLAT, NLON), jnp.float32, -0.4, 0.4) * shard_levels(keys[4], (2, LEV, NLAT, NLON), ((2, 16), (3, 64)), -0.4, 0.0), -0.4, 0.4),
        "sea_mask": place_ends((jax.random.randint(keys[5], (NLAT, NLON), 0, 10) < 7).astype(jnp.int32), jax.random.fold_in(keys[5], 1), 0, 1),
        "observed": gaussian(keys[6], (2, 3, LEV, NLAT, NLON), 1.0, 6.0, ((3, 16), (4, 64)), jnp.float32),
        "loc_reach": draw_loc_reach(jax.random.fold_in(keys[8], 71), 0),
    }


diffusion_number = 0.2

def loc_weights(loc_reach):
    distance = jnp.arange(REACH + 1).astype(jnp.float32)
    limits = loc_reach.astype(jnp.float32)[:, None] + 1.0
    return jnp.maximum(0.0, 1.0 - distance[None, :] / limits)

def band_roll(field, offset):
    lead = field.shape[:-2]
    banded = field.reshape(lead + (BANDS, CLAT, NLON))
    rolled = jnp.roll(banded, offset, axis=-3)
    return rolled.reshape(field.shape)

def band_mix(field, weight_row):
    summed = weight_row[:, 0][:, None, None, None, None] * field
    for distance in range(1, REACH + 1):
        factor = weight_row[:, distance][:, None, None, None, None]
        summed = summed + factor * band_roll(field, distance) + factor * band_roll(field, -distance)
    return summed

def neighbours(field):
    east = jnp.roll(field, -1, axis=-1)
    west = jnp.roll(field, 1, axis=-1)
    config = [(0, 0)] * (field.ndim - 2) + [(1, 1), (0, 0)]
    padded = jnp.pad(field, config)
    north = padded[..., 2:, :]
    south = padded[..., :-2, :]
    return (east, west, north, south)

def tangent(field, coeffs, sea):
    east_c, west_c, north_c, south_c = coeffs
    east, west, north, south = neighbours(field)
    centre = 1.0 - 4.0 * diffusion_number
    return sea * (centre * field + east_c * east + west_c * west + north_c * north + south_c * south)

def adjoint(field, coeffs, sea):
    east_c, west_c, north_c, south_c = coeffs
    masked = sea * field
    centre = 1.0 - 4.0 * diffusion_number
    summed = centre * masked + neighbours(east_c * masked)[1]
    summed = summed + neighbours(west_c * masked)[0]
    summed = summed + neighbours(north_c * masked)[3]
    summed = summed + neighbours(south_c * masked)[2]
    return summed

def reference(ens_control, perturbations, zonal_control, spread, currents, sea_mask, observed, loc_reach):
    scale = 1.0 / math.sqrt(MEMB - 1)
    zscale = 1.0 / math.sqrt(NLON)
    group = MEMB // NBLK
    weights = jnp.repeat(loc_weights(loc_reach), group, axis=0).reshape(NBLK, group, REACH + 1)
    control_blocks = ens_control.reshape((NBLK, group) + ens_control.shape[1:])
    pert_blocks = perturbations.reshape((NBLK, group) + perturbations.shape[1:])

    def forward_block(items):
        control_part, pert_part, weight_row = items
        mixed = band_mix(control_part.astype(jnp.float32), weight_row)
        return lax.optimization_barrier(jnp.sum(pert_part.astype(jnp.float32) * mixed, axis=0))
    ens_part = lax.optimization_barrier(jnp.sum(lax.map(forward_block, (control_blocks, pert_blocks, weights)), axis=0))
    start = ens_part * scale + spread * zonal_control[..., None] * zscale
    sea = sea_mask.astype(jnp.float32)
    zonal_flow = currents[0]
    merid_flow = currents[1]
    coeffs = (diffusion_number - 0.5 * zonal_flow, diffusion_number + 0.5 * zonal_flow, diffusion_number - 0.5 * merid_flow, diffusion_number + 0.5 * merid_flow)
    first = tangent(start, coeffs, sea)
    second = tangent(first, coeffs, sea)
    weighted = first - observed[0] + adjoint(second - observed[1], coeffs, sea)
    sensitivity = adjoint(weighted, coeffs, sea)

    def backward_block(items):
        pert_part, weight_row = items
        products = lax.optimization_barrier((pert_part.astype(jnp.float32) * sensitivity * scale).astype(jnp.bfloat16))
        return band_mix(products.astype(jnp.float32), weight_row)
    ens_grad = lax.map(backward_block, (pert_blocks, weights)).reshape(ens_control.shape)
    zonal_grad = zonal_control + lax.optimization_barrier(jnp.sum(spread * sensitivity, axis=-1)) * zscale
    return (ens_grad, zonal_grad)
```

```python
import math

import jax
import jax.numpy as jnp
from jax import lax
from jax.sharding import PartitionSpec as P

NU = 0.2
HALO = 4


def cyc(value, axis, distance):
    peers = lax.axis_size(axis)
    return lax.ppermute(value, axis, [((i - distance) % peers, i) for i in range(peers)])


def open_step(value, axis, distance):
    peers = lax.axis_size(axis)
    route = [(i - distance, i) for i in range(peers) if 0 <= i - distance < peers]
    return lax.ppermute(value, axis, route)


def widen_lon(value):
    last = value[..., value.shape[-1] - HALO :]
    leading = value[..., :HALO]
    return jnp.concatenate([cyc(last, "lon", 1), value, cyc(leading, "lon", -1)], axis=-1)


def crop(value, ring):
    return value[..., ring : value.shape[-2] - ring, ring : value.shape[-1] - ring]


def sides(value):
    inner = value[..., 1:-1, 1:-1]
    east = value[..., 1:-1, 2:]
    west = value[..., 1:-1, :-2]
    north = value[..., 2:, 1:-1]
    south = value[..., :-2, 1:-1]
    return inner, east, west, north, south


def tangent(field, flow, sea):
    cu, cv = crop(flow[0], 1), crop(flow[1], 1)
    inner, east, west, north, south = sides(field)
    return crop(sea, 1) * (
        (1.0 - 4.0 * NU) * inner
        + (NU - 0.5 * cu) * east
        + (NU + 0.5 * cu) * west
        + (NU - 0.5 * cv) * north
        + (NU + 0.5 * cv) * south
    )


def adjoint(field, flow, sea):
    masked = sea * field
    summed = (1.0 - 4.0 * NU) * sides(masked)[0]
    summed = summed + sides((NU - 0.5 * flow[0]) * masked)[2]
    summed = summed + sides((NU + 0.5 * flow[0]) * masked)[1]
    summed = summed + sides((NU - 0.5 * flow[1]) * masked)[4]
    summed = summed + sides((NU + 0.5 * flow[1]) * masked)[3]
    return summed


def local(
    ens_control, perturbations, zonal_control, spread, currents, sea_mask, observed, loc_reach
):
    bands = lax.axis_size("lat")
    members = ens_control.shape[0]
    group = members // loc_reach.shape[0]
    rows = spread.shape[2]
    scale = 1.0 / math.sqrt(members - 1)
    zscale = 1.0 / math.sqrt(ens_control.shape[4] * lax.axis_size("lon"))
    distance_axis = jnp.arange(3).astype(jnp.float32)
    limits = loc_reach.astype(jnp.float32)[:, None] + 1.0
    block_weights = jnp.maximum(0.0, 1.0 - distance_axis[None, :] / limits)
    weights = jnp.repeat(block_weights, group, axis=0)

    pert = {0: perturbations}
    for o in (1, -1, 2, -2):
        pert[o] = cyc(perturbations, "lat", -o)

    sea_f = sea_mask.astype(jnp.float32)
    inputs = jnp.concatenate(
        [
            currents.reshape((-1,) + currents.shape[-2:]),
            observed.reshape((-1,) + observed.shape[-2:]),
            sea_f[None],
        ],
        axis=0,
    )
    inputs = widen_lon(inputs)
    inputs = jnp.concatenate(
        [open_step(inputs, "lat", 1), inputs, open_step(inputs, "lat", -1)], axis=-2
    )
    ncur = currents.shape[0] * currents.shape[1]
    flow = inputs[:ncur].reshape(currents.shape[:2] + inputs.shape[1:])
    obs = inputs[ncur:-1].reshape(observed.shape[:3] + inputs.shape[1:])
    sea = inputs[-1]

    def pair(o):
        w = weights[:, abs(o)][:, None, None, None, None] * scale
        return jnp.sum(
            w * pert[o].astype(jnp.float32) * ens_control.astype(jnp.float32), axis=0
        )

    part = {o: pair(o) for o in range(-2, 3)}
    part[0] = part[0] + spread * zonal_control[..., None] * zscale
    sums = {s: part[s] for s in (-1, 0, 1)}
    for d in (1, -1, 2, -2, 3, -3):
        which = [s for s in (-1, 0, 1) if abs(d + s) <= 2]
        moved = cyc(jnp.stack([part[d + s] for s in which]), "lat", d)
        for n, s in enumerate(which):
            sums[s] = sums[s] + moved[n]
    band = lax.axis_index("lat")
    south = jnp.where(band > 0, sums[-1], 0.0)
    north = jnp.where(band < bands - 1, sums[1], 0.0)
    start = jnp.concatenate([south, sums[0], north], axis=2)
    start = widen_lon(start)

    first = tangent(start, flow, sea)
    second = tangent(first, crop(flow, 1), crop(sea, 1))
    weighted = crop(first, 2) - crop(obs[0], 3) + adjoint(
        second - crop(obs[1], 2), crop(flow, 2), crop(sea, 2)
    )
    sensitivity = adjoint(weighted, crop(flow, 3), crop(sea, 3))

    grad = None
    for o in (0, 1, -1, 2, -2):
        sens = sensitivity if o == 0 else cyc(sensitivity, "lat", -o)
        product = (pert[o].astype(jnp.float32) * sens * scale).astype(jnp.bfloat16)
        term = weights[:, abs(o)][:, None, None, None, None] * product.astype(jnp.float32)
        grad = term if grad is None else grad + term
    zonal_part = jnp.sum(spread * sensitivity, axis=3)
    summed = lax.psum(zonal_part.reshape(1, -1), "lon").reshape(zonal_part.shape)
    zonal_grad = zonal_control + summed * zscale
    return grad, zonal_grad


def solution(mesh):
    return jax.shard_map(
        local,
        mesh=mesh,
        in_specs=(
            P(None, None, None, "lat", "lon"),
            P(None, None, None, "lat", "lon"),
            P(None, None, "lat"),
            P(None, None, "lat", "lon"),
            P(None, None, "lat", "lon"),
            P("lat", "lon"),
            P(None, None, None, "lat", "lon"),
            P(),
        ),
        out_specs=(P(None, None, None, "lat", "lon"), P(None, None, "lat")),
        check_vma=False,
    )
```

```python
import math

import jax
import jax.numpy as jnp
from jax import lax
from jax.experimental import pallas as pl
from jax.experimental.pallas import tpu as pltpu
from jax.sharding import PartitionSpec as P

NU = 0.2
REACH = 2
HALO = 4
PAD = 16
LANES = 128
PACK = LANES // HALO
LEAST = 3
FEW = 4
VMEM = pltpu.MemorySpace.VMEM
SMEM = pltpu.MemorySpace.SMEM


def shift(value, axis, distance):
    peers = lax.axis_size(axis)
    return lax.ppermute(value, axis, [((i - distance) % peers, i) for i in range(peers)])


def pairs_kernel(order, count, weight, own, control, up1, down1, up2, down2, out):
    i = pl.program_id(0)

    def add(slot, source, w):
        total = None
        for m in range(control.shape[1]):
            term = source[0, m].astype(jnp.float32) * control[0, m].astype(jnp.float32)
            total = term if total is None else total + term
        out[slot] += w * total

    @pl.when(i == 0)
    def _():
        out[...] = jnp.zeros(out.shape, out.dtype)

    add(2, own, weight[i, 0])

    @pl.when(i < count[0])
    def _():
        add(3, up1, weight[i, 1])
        add(1, down1, weight[i, 1])

    @pl.when(i < count[1])
    def _():
        add(4, up2, weight[i, 2])
        add(0, down2, weight[i, 2])


def mixed_kernel(rank, weight, sens, own, up1, down1, up2, down2, out):
    j = pl.program_id(0)

    def product(source, slot, m):
        value = source[0, m].astype(jnp.float32) * sens[slot]
        return value.astype(jnp.bfloat16).astype(jnp.float32)

    for m in range(own.shape[1]):
        out[0, m] = weight[j, 0] * product(own, 2, m)

    @pl.when(weight[j, 1] > 0.0)
    def _():
        for m in range(own.shape[1]):
            out[0, m] += weight[j, 1] * (product(up1, 3, m) + product(down1, 1, m))

    @pl.when(weight[j, 2] > 0.0)
    def _():
        for m in range(own.shape[1]):
            out[0, m] += weight[j, 2] * (product(up2, 4, m) + product(down2, 0, m))


def lane(shape):
    return lax.broadcasted_iota(jnp.int32, shape, len(shape) - 1)


def gather_kernel(inside, part, inputs, r1, m1, r2, m2, r3, m3, field, west_edge, east_edge):
    n = r3.shape[0]
    south = part[n : 2 * n] + r1[:n] + m1[:n] + r2[:n] + r3[...]
    mid = part[2 * n : 3 * n] + r1[n : 2 * n] + m1[n : 2 * n] + r2[n : 2 * n] + m2[:n]
    north = part[3 * n : 4 * n] + r1[2 * n : 3 * n] + m1[2 * n : 3 * n] + m2[n : 2 * n] + m3[...]
    low, high = inside[0] > 0, inside[1] > 0
    field[:, 12:PAD] = jnp.zeros((field.shape[0], PAD - 12, LANES), jnp.float32)
    field[:n, 0:4] = jnp.where(low, south, 0.0)
    field[:n, 4:8] = mid
    field[:n, 8:12] = jnp.where(high, north, 0.0)
    field[n:, 0:4] = jnp.where(low, r1[3 * n :], 0.0)
    field[n:, 4:8] = inputs[...]
    field[n:, 8:12] = jnp.where(high, m1[3 * n :], 0.0)
    spot = lane((PAD, LANES)) // HALO
    for g in range(west_edge.shape[0]):
        west = jnp.zeros((PAD, LANES), jnp.float32)
        east = jnp.zeros((PAD, LANES), jnp.float32)
        for k in range(min(PACK, field.shape[0] - g * PACK)):
            value = field[g * PACK + k]
            at = HALO * k
            west = jnp.where(spot == k, pltpu.roll(value, at, 1) if at else value, west)
            east = jnp.where(spot == k, pltpu.roll(value, (at + HALO) % LANES, 1) if at + HALO < LANES else value, east)
        west_edge[g] = west
        east_edge[g] = east


def stencil_kernel(field, from_east, from_west, out):
    n = out.shape[0]
    cols = lane((PAD, LANES))

    def turn(value, amount):
        return pltpu.roll(value, amount % LANES, 1) if amount % LANES else value

    def wide(i):
        g, at = i // PACK, HALO * (i % PACK)
        right = turn(from_east[g], -at)
        left = turn(from_west[g], -at - HALO)
        beside = jnp.where(cols < HALO, right, jnp.where(cols >= LANES - HALO, left, 0.0))
        return field[i], beside

    def at_west(v):
        a, b = pltpu.roll(v[0], 1, 1), pltpu.roll(v[1], 1, 1)
        return jnp.where(cols == 0, b, a), jnp.where(cols == 0, a, b)

    def at_east(v):
        a, b = pltpu.roll(v[0], LANES - 1, 1), pltpu.roll(v[1], LANES - 1, 1)
        return jnp.where(cols == LANES - 1, b, a), jnp.where(cols == LANES - 1, a, b)

    def at_north(v):
        return tuple(pltpu.roll(x, PAD - 1, 0) for x in v)

    def at_south(v):
        return tuple(pltpu.roll(x, 1, 0) for x in v)

    def each(f, *vs):
        return tuple(f(*xs) for xs in zip(*vs))

    def mul(a, b):
        return each(lambda x, y: x * y, a, b)

    def sub(a, b):
        return each(lambda x, y: x - y, a, b)

    def total(*vs):
        return each(lambda *xs: sum(xs[1:], xs[0]), *vs)

    centre = 1.0 - 4.0 * NU
    levels = n // 3
    sea = wide(field.shape[0] - 1)
    for l in range(levels):
        cu, cv = wide(n + l), wide(n + levels + l)
        east_c = each(lambda x: NU - 0.5 * x, cu)
        west_c = each(lambda x: NU + 0.5 * x, cu)
        north_c = each(lambda x: NU - 0.5 * x, cv)
        south_c = each(lambda x: NU + 0.5 * x, cv)

        def tangent(f):
            return mul(
                sea,
                total(
                    each(lambda x: centre * x, f),
                    mul(east_c, at_east(f)),
                    mul(west_c, at_west(f)),
                    mul(north_c, at_north(f)),
                    mul(south_c, at_south(f)),
                ),
            )

        def adjoint(f):
            z = mul(sea, f)
            return total(
                each(lambda x: centre * x, z),
                at_west(mul(east_c, z)),
                at_east(mul(west_c, z)),
                at_south(mul(north_c, z)),
                at_north(mul(south_c, z)),
            )

        for t in range(3):
            i = t * levels + l
            first = tangent(wide(i))
            second = tangent(first)
            near = wide(n + 2 * levels + i)
            later = wide(n + 2 * levels + n + i)
            weighted = total(sub(first, near), adjoint(sub(second, later)))
            out[i] = adjoint(weighted)[0][4:8]


def whole():
    return pl.BlockSpec(memory_space=VMEM)


def local(
    ens_control, perturbations, zonal_control, spread, currents, sea_mask, observed, loc_reach
):
    bands = lax.axis_size("lat")
    slabs = lax.axis_size("lon")
    members, tracers, levels, rows, columns = ens_control.shape
    blocks = loc_reach.shape[0]
    group = members // blocks
    cells = tracers * levels * rows
    scale = 1.0 / math.sqrt(members - 1)
    zscale = 1.0 / math.sqrt(columns * slabs)
    limits = loc_reach.astype(jnp.float32)[:, None] + 1.0
    weights = jnp.maximum(0.0, 1.0 - jnp.arange(REACH + 1).astype(jnp.float32)[None, :] / limits)

    mine, other = loc_reach[:, None], loc_reach[None, :]
    index = jnp.arange(blocks)
    ahead = (other > mine) | ((other == mine) & (index[None, :] < index[:, None]))
    rank = jnp.sum(ahead.astype(jnp.int32), axis=1)
    placed = rank[None, :] == index[:, None]
    order = jnp.sum(jnp.where(placed, index[None, :], 0), axis=1).astype(jnp.int32)
    sorted_weights = jnp.sum(jnp.where(placed[:, :, None], weights[None], 0.0), axis=1)
    count1 = jnp.sum((loc_reach >= 1).astype(jnp.int32))
    count2 = jnp.sum((loc_reach >= 2).astype(jnp.int32))

    own = perturbations.reshape(blocks, group, cells, columns)
    control = ens_control.reshape(blocks, group, cells, columns)
    sending = lax.optimization_barrier(jnp.take(own, order, axis=0, mode="clip"))
    most = blocks - 1

    def exchange(near, far):
        def run(block):
            got = []
            for distance, n in ((-1, near), (1, near), (-2, far), (2, far)):
                moved = shift(block[:n], "lat", distance)
                rest = jnp.zeros((most - n,) + block.shape[1:], block.dtype)
                got.append(jnp.concatenate([moved, rest], axis=0) if n < most else moved)
            return tuple(got)

        return run

    sizes, starts = [], []
    for near in range(LEAST, most + 1):
        starts.append(len(sizes))
        far = list(range(2, min(near, FEW) + 1))
        sizes += [(near, n) for n in far + [near] * (near > FEW)]
    cases = [exchange(near, far) for near, far in sizes]
    near = jnp.maximum(count1, LEAST)
    case = jnp.clip(count2 - 2, 0, FEW - 1)
    for n, first in enumerate(starts):
        case = case + jnp.where(near == LEAST + n, first, 0)
    up1, down1, up2, down2 = lax.optimization_barrier(lax.switch(case, cases, sending))

    block = (1, group, cells, columns)
    place = pl.BlockSpec(block, lambda i, order, count: (order[i], 0, 0, 0))
    got = pl.BlockSpec(block, lambda i, order, count: (jnp.minimum(i, most - 1), 0, 0, 0))
    part = pl.pallas_call(
        pairs_kernel,
        grid_spec=pltpu.PrefetchScalarGridSpec(
            num_scalar_prefetch=2,
            grid=(blocks,),
            in_specs=[pl.BlockSpec(memory_space=SMEM), place, place, got, got, got, got],
            out_specs=pl.BlockSpec((5, cells, columns), lambda i, order, count: (0, 0, 0)),
        ),
        out_shape=jax.ShapeDtypeStruct((5, cells, columns), jnp.float32),
        name="pairs",
    )(order, jnp.stack([count1, count2]), sorted_weights * scale, own, control, up1, down1, up2, down2)

    items = tracers * levels
    part = part.reshape(5, items, rows, columns)
    prior = (spread * zonal_control[..., None] * zscale).reshape(items, rows, columns)
    part = jnp.concatenate([part[:2], (part[2] + prior)[None], part[3:]], axis=0)
    part = part.reshape(5 * items, rows, columns)
    inputs = jnp.concatenate(
        [
            currents.reshape(-1, rows, columns),
            observed.reshape(-1, rows, columns),
            sea_mask.astype(jnp.float32)[None],
        ],
        axis=0,
    )
    r3 = shift(part[4 * items :], "lat", 3)
    m3 = shift(part[:items], "lat", -3)
    r2 = shift(part[3 * items :], "lat", 2)
    m2 = shift(part[: 2 * items], "lat", -2)
    r1 = shift(jnp.concatenate([part[2 * items :], inputs], axis=0), "lat", 1)
    m1 = shift(jnp.concatenate([part[: 3 * items], inputs], axis=0), "lat", -1)
    band = lax.axis_index("lat")
    inside = jnp.stack([band > 0, band < bands - 1]).astype(jnp.int32)
    total = items + inputs.shape[0]
    packs = -(-total // PACK)
    field, west_edge, east_edge = pl.pallas_call(
        gather_kernel,
        in_specs=[pl.BlockSpec(memory_space=SMEM)] + [whole()] * 8,
        out_specs=[whole()] * 3,
        out_shape=[
            jax.ShapeDtypeStruct((total, PAD, columns), jnp.float32),
            jax.ShapeDtypeStruct((packs, PAD, columns), jnp.float32),
            jax.ShapeDtypeStruct((packs, PAD, columns), jnp.float32),
        ],
        name="gather",
    )(inside, part, inputs, r1, m1, r2, m2, r3, m3)
    from_east = shift(west_edge, "lon", -1)
    from_west = shift(east_edge, "lon", 1)
    sensitivity = pl.pallas_call(
        stencil_kernel,
        in_specs=[whole()] * 3,
        out_specs=whole(),
        out_shape=jax.ShapeDtypeStruct((items, rows, columns), jnp.float32),
        name="stencil",
    )(field, from_east, from_west)

    down = [shift(sensitivity, "lat", d) for d in (2, 1)]
    up = [shift(sensitivity, "lat", -d) for d in (1, 2)]
    sens = jnp.stack(down + [sensitivity] + up).reshape(5, cells, columns) * scale

    zonal_part = jnp.sum(spread.reshape(cells, columns) * sensitivity.reshape(cells, columns), axis=1)
    spread_out = jnp.broadcast_to(zonal_part[None], (slabs, cells))
    everyone = lax.all_to_all(spread_out, "lon", 0, 0, tiled=True)
    summed = jnp.sum(everyone, axis=0).reshape(zonal_control.shape)
    zonal_grad = zonal_control + summed * zscale

    here = pl.BlockSpec(block, lambda j, rank: (j, 0, 0, 0))
    taken = pl.BlockSpec(block, lambda j, rank: (jnp.minimum(rank[j], most - 1), 0, 0, 0))
    grad = pl.pallas_call(
        mixed_kernel,
        grid_spec=pltpu.PrefetchScalarGridSpec(
            num_scalar_prefetch=1,
            grid=(blocks,),
            in_specs=[
                pl.BlockSpec(memory_space=SMEM),
                pl.BlockSpec((5, cells, columns), lambda j, rank: (0, 0, 0)),
                here,
                taken,
                taken,
                taken,
                taken,
            ],
            out_specs=here,
        ),
        out_shape=jax.ShapeDtypeStruct((blocks, group, cells, columns), jnp.float32),
        name="mixed",
    )(rank, weights, sens, own, up1, down1, up2, down2)
    return grad.reshape(ens_control.shape), zonal_grad


def solution(mesh):
    return jax.shard_map(
        local,
        mesh=mesh,
        in_specs=(
            P(None, None, None, "lat", "lon"),
            P(None, None, None, "lat", "lon"),
            P(None, None, "lat"),
            P(None, None, "lat", "lon"),
            P(None, None, "lat", "lon"),
            P("lat", "lon"),
            P(None, None, None, "lat", "lon"),
            P(),
        ),
        out_specs=(P(None, None, None, "lat", "lon"), P(None, None, "lat")),
        check_vma=False,
    )
```

```python
import functools
import math

import jax
import jax.numpy as jnp
from jax import lax
from jax.experimental import pallas as pl
from jax.experimental.pallas import tpu as pltpu
from jax.sharding import PartitionSpec as P


NU = 0.2
REACH = 2
HALO = 4
PAD = 16
LANES = 128
PACK = LANES // HALO
LEAST = 3
FEW = 4
VMEM = pltpu.MemorySpace.VMEM
SMEM = pltpu.MemorySpace.SMEM


def shift(value, axis, distance):
    peers = lax.axis_size(axis)
    return lax.ppermute(value, axis, [((i - distance) % peers, i) for i in range(peers)])


def sort_kernel(reach, own, out, order, rank, case, sems):
    blocks = own.shape[0]
    for j in range(blocks):
        place = jnp.int32(0)
        for i in range(blocks):
            if i != j:
                ahead = reach[i] >= reach[j] if i < j else reach[i] > reach[j]
                place = place + ahead.astype(jnp.int32)
        rank[j] = place
        order[place] = j
        pltpu.make_async_copy(own.at[j], out.at[place], sems.at[j]).start()
    near, far = jnp.int32(0), jnp.int32(0)
    for j in range(blocks):
        near = near + (reach[j] >= 1).astype(jnp.int32)
        far = far + (reach[j] >= 2).astype(jnp.int32)
    near = jnp.maximum(near, LEAST)
    chosen = jnp.clip(far - 2, 0, FEW - 1)
    for n, first in enumerate(send_sizes(blocks - 1)[1]):
        chosen = chosen + jnp.where(near == LEAST + n, first, 0)
    case[0] = chosen
    for j in range(blocks):
        pltpu.make_async_copy(own.at[j], out.at[rank[j]], sems.at[j]).wait()


def send_sizes(most):
    sizes, starts = [], []
    for near in range(LEAST, most + 1):
        starts.append(len(sizes))
        far = list(range(2, min(near, FEW) + 1))
        sizes += [(near, n) for n in far + [near] * (near > FEW)]
    return sizes, starts


def weight_of(reach, distance):
    limit = jnp.full((1, LANES), reach.astype(jnp.float32)) + 1.0
    return jnp.maximum(0.0, 1.0 - distance / limit)


def pairs_kernel(
    order, reach, own, control, up1, down1, up2, down2, prior, zonal, flow, seen, sea,
    to_up1, to_down1, to_up2, to_down2, to_up3, to_down3, sums, *, scale, zscale
):
    i = pl.program_id(0)
    here = reach[order[i]]
    n = sums.shape[1]

    def added(source):
        total = None
        for m in range(control.shape[1]):
            term = source[0, m].astype(jnp.float32) * control[0, m].astype(jnp.float32)
            total = term if total is None else total + term
        return total

    @pl.when(i == 0)
    def _():
        sums[...] = jnp.zeros(sums.shape, sums.dtype)

    sums[2] += weight_of(here, 0.0) * added(own)

    @pl.when(here >= 1)
    def _():
        w = weight_of(here, 1.0)
        sums[3] += w * added(up1)
        sums[1] += w * added(down1)

    @pl.when(here >= 2)
    def _():
        w = weight_of(here, 2.0)
        sums[4] += w * added(up2)
        sums[0] += w * added(down2)

    @pl.when(i == pl.num_programs(0) - 1)
    def _():
        part = [sums[o] * scale for o in range(5)]
        part[2] = part[2] + prior[...] * zonal[...] * zscale
        for k in range(3):
            to_up1[k * n : (k + 1) * n] = part[2 + k]
            to_down1[k * n : (k + 1) * n] = part[k]
        for k in range(2):
            to_up2[k * n : (k + 1) * n] = part[3 + k]
            to_down2[k * n : (k + 1) * n] = part[k]
        to_up3[...] = part[4]
        to_down3[...] = part[0]
        for out in (to_up1, to_down1):
            at = 3 * n
            for source in (flow, seen):
                out[at : at + source.shape[0]] = source[...]
                at += source.shape[0]
            out[at : at + sea.shape[0]] = sea[...].astype(jnp.float32)


def mixed_kernel(rank, reach, down2_s, down1_s, own_s, up1_s, up2_s, own, up1, down1, up2, down2, out, *, scale):
    here = reach[pl.program_id(0)]
    pieces = [[(own, own_s)], [(up1, up1_s), (down1, down1_s)], [(up2, up2_s), (down2, down2_s)]]

    def run(last):
        weights = [weight_of(here, float(d)) for d in range(last + 1)]
        for m in range(own.shape[1]):
            total = None
            for d in range(last + 1):
                near = None
                for source, sens in pieces[d]:
                    value = source[0, m].astype(jnp.float32) * (sens[...] * scale)
                    value = value.astype(jnp.bfloat16).astype(jnp.float32)
                    near = value if near is None else near + value
                near = weights[d] * near
                total = near if total is None else total + near
            out[0, m] = total

    for d in range(REACH + 1):
        pl.when(here >= d if d == REACH else here == d)(lambda d=d: run(d))


def lane(shape):
    return lax.broadcasted_iota(jnp.int32, shape, len(shape) - 1)


def gather_kernel(inside, up, down, r1, m1, r2, m2, r3, m3, field, west_edge, east_edge):
    n = r3.shape[0]
    low, high = inside[0] > 0, inside[1] > 0
    south = down[n : 2 * n] + r1[:n] + m1[:n] + r2[:n] + r3[...]
    mid = up[:n] + r1[n : 2 * n] + m1[n : 2 * n] + r2[n : 2 * n] + m2[:n]
    north = up[n : 2 * n] + r1[2 * n : 3 * n] + m1[2 * n : 3 * n] + m2[n : 2 * n] + m3[...]
    field[:, 12:PAD] = jnp.zeros((field.shape[0], PAD - 12, LANES), jnp.float32)
    south, north = jnp.where(low, south, 0.0), jnp.where(high, north, 0.0)
    for i in range(n // 4):
        field[i, 0:4] = south[4 * i : 4 * i + 4]
        field[i, 4:8] = mid[4 * i : 4 * i + 4]
        field[i, 8:12] = north[4 * i : 4 * i + 4]
    for i in range(n // 4, field.shape[0]):
        at = pl.ds(2 * n + 4 * i, 4)
        field[i, 0:4] = jnp.where(low, r1[at], 0.0)
        field[i, 4:8] = up[at]
        field[i, 8:12] = jnp.where(high, m1[at], 0.0)
    spot = lane((PAD, LANES)) // HALO
    for g in range(west_edge.shape[0]):
        west = jnp.zeros((PAD, LANES), jnp.float32)
        east = jnp.zeros((PAD, LANES), jnp.float32)
        for k in range(min(PACK, field.shape[0] - g * PACK)):
            value = field[g * PACK + k]
            at = HALO * k
            west = jnp.where(spot == k, pltpu.roll(value, at, 1) if at else value, west)
            east = jnp.where(spot == k, pltpu.roll(value, (at + HALO) % LANES, 1) if at + HALO < LANES else value, east)
        west_edge[g] = west
        east_edge[g] = east


def stencil_kernel(field, from_east, from_west, out):
    n = out.shape[0] // 4
    cols = lane((PAD, LANES))

    def turn(value, amount):
        return pltpu.roll(value, amount % LANES, 1) if amount % LANES else value

    def wide(i):
        g, at = i // PACK, HALO * (i % PACK)
        right = turn(from_east[g], -at)
        left = turn(from_west[g], -at - HALO)
        beside = jnp.where(cols < HALO, right, jnp.where(cols >= LANES - HALO, left, 0.0))
        return field[i], beside

    def at_west(v):
        a, b = pltpu.roll(v[0], 1, 1), pltpu.roll(v[1], 1, 1)
        return jnp.where(cols == 0, b, a), jnp.where(cols == 0, a, b)

    def at_east(v):
        a, b = pltpu.roll(v[0], LANES - 1, 1), pltpu.roll(v[1], LANES - 1, 1)
        return jnp.where(cols == LANES - 1, b, a), jnp.where(cols == LANES - 1, a, b)

    def at_north(v):
        return tuple(pltpu.roll(x, PAD - 1, 0) for x in v)

    def at_south(v):
        return tuple(pltpu.roll(x, 1, 0) for x in v)

    def each(f, *vs):
        return tuple(f(*xs) for xs in zip(*vs))

    def mul(a, b):
        return each(lambda x, y: x * y, a, b)

    def sub(a, b):
        return each(lambda x, y: x - y, a, b)

    def total(*vs):
        return each(lambda *xs: sum(xs[1:], xs[0]), *vs)

    centre = 1.0 - 4.0 * NU
    levels = n // 3
    sea = wide(field.shape[0] - 1)
    for l in range(levels):
        cu, cv = wide(n + l), wide(n + levels + l)
        east_c = each(lambda x: NU - 0.5 * x, cu)
        west_c = each(lambda x: NU + 0.5 * x, cu)
        north_c = each(lambda x: NU - 0.5 * x, cv)
        south_c = each(lambda x: NU + 0.5 * x, cv)

        def tangent(f):
            return mul(
                sea,
                total(
                    each(lambda x: centre * x, f),
                    mul(east_c, at_east(f)),
                    mul(west_c, at_west(f)),
                    mul(north_c, at_north(f)),
                    mul(south_c, at_south(f)),
                ),
            )

        def adjoint(f):
            z = mul(sea, f)
            return total(
                each(lambda x: centre * x, z),
                at_west(mul(east_c, z)),
                at_east(mul(west_c, z)),
                at_south(mul(north_c, z)),
                at_north(mul(south_c, z)),
            )

        for t in range(3):
            i = t * levels + l
            first = tangent(wide(i))
            second = tangent(first)
            near = wide(n + 2 * levels + i)
            later = wide(n + 2 * levels + n + i)
            weighted = total(sub(first, near), adjoint(sub(second, later)))
            out[4 * i : 4 * i + 4] = adjoint(weighted)[0][4:8]


def whole():
    return pl.BlockSpec(memory_space=VMEM)


def local(
    ens_control, perturbations, zonal_control, spread, currents, sea_mask, observed, loc_reach
):
    bands = lax.axis_size("lat")
    slabs = lax.axis_size("lon")
    members, tracers, levels, rows, columns = ens_control.shape
    blocks = loc_reach.shape[0]
    group = members // blocks
    cells = tracers * levels * rows
    scale = 1.0 / math.sqrt(members - 1)
    zscale = 1.0 / math.sqrt(columns * slabs)
    own = perturbations.reshape(blocks, group, cells, columns)
    control = ens_control.reshape(blocks, group, cells, columns)
    most = blocks - 1
    place = pl.BlockSpec(memory_space=pl.ANY)
    small = pl.BlockSpec(memory_space=SMEM)
    sending, order, rank, case = pl.pallas_call(
        sort_kernel,
        in_specs=[small, place],
        out_specs=[place, small, small, small],
        out_shape=[
            jax.ShapeDtypeStruct(own.shape, own.dtype),
            jax.ShapeDtypeStruct((blocks,), jnp.int32),
            jax.ShapeDtypeStruct((blocks,), jnp.int32),
            jax.ShapeDtypeStruct((1,), jnp.int32),
        ],
        scratch_shapes=[pltpu.SemaphoreType.DMA((blocks,))],
        name="sort",
    )(loc_reach, own)

    def exchange(near, far):
        def run(block):
            got = []
            for distance, n in ((-1, near), (1, near), (-2, far), (2, far)):
                moved = shift(block[:n], "lat", distance)
                rest = jnp.zeros((most - n,) + block.shape[1:], block.dtype)
                got.append(jnp.concatenate([moved, rest], axis=0) if n < most else moved)
            return tuple(got)

        return run

    cases = [exchange(near, far) for near, far in send_sizes(most)[0]]
    up1, down1, up2, down2 = lax.optimization_barrier(lax.switch(case[0], cases, sending))

    items = tracers * levels
    lines = [x.reshape(-1, columns) for x in (spread, currents, observed, sea_mask)]
    zonal = jnp.broadcast_to(zonal_control.reshape(cells, 1), (cells, columns))
    beside = sum(x.shape[0] for x in lines[1:])
    messages = [3 * cells + beside] * 2 + [2 * cells] * 2 + [cells] * 2

    def fixed(shape):
        return pl.BlockSpec(shape, lambda i, *_: (0,) * len(shape))

    block = (1, group, cells, columns)
    sorted_block = pl.BlockSpec(block, lambda i, order, reach: (order[i], 0, 0, 0))
    got = pl.BlockSpec(block, lambda i, order, reach: (jnp.minimum(i, most - 1), 0, 0, 0))
    to_up1, to_down1, to_up2, to_down2, to_up3, to_down3 = pl.pallas_call(
        functools.partial(pairs_kernel, scale=scale, zscale=zscale),
        grid_spec=pltpu.PrefetchScalarGridSpec(
            num_scalar_prefetch=2,
            grid=(blocks,),
            in_specs=[sorted_block] * 2
            + [got] * 4
            + [fixed(x.shape) for x in (lines[0], zonal, *lines[1:])],
            out_specs=[fixed((n, columns)) for n in messages],
            scratch_shapes=[pltpu.VMEM((5, cells, columns), jnp.float32)],
        ),
        out_shape=[jax.ShapeDtypeStruct((n, columns), jnp.float32) for n in messages],
        name="pairs",
    )(order, loc_reach, own, control, up1, down1, up2, down2, lines[0], zonal, *lines[1:])

    r1, m1 = shift(to_up1, "lat", 1), shift(to_down1, "lat", -1)
    r2, m2 = shift(to_up2, "lat", 2), shift(to_down2, "lat", -2)
    r3, m3 = shift(to_up3, "lat", 3), shift(to_down3, "lat", -3)
    band = lax.axis_index("lat")
    inside = jnp.stack([band > 0, band < bands - 1]).astype(jnp.int32)
    total = items + beside // rows
    packs = -(-total // PACK)
    field, west_edge, east_edge = pl.pallas_call(
        gather_kernel,
        in_specs=[small] + [whole()] * 8,
        out_specs=[whole()] * 3,
        out_shape=[
            jax.ShapeDtypeStruct((total, PAD, columns), jnp.float32),
            jax.ShapeDtypeStruct((packs, PAD, columns), jnp.float32),
            jax.ShapeDtypeStruct((packs, PAD, columns), jnp.float32),
        ],
        name="gather",
    )(inside, to_up1, to_down1, r1, m1, r2, m2, r3, m3)
    from_east = shift(west_edge, "lon", -1)
    from_west = shift(east_edge, "lon", 1)
    sensitivity = pl.pallas_call(
        stencil_kernel,
        in_specs=[whole()] * 3,
        out_specs=whole(),
        out_shape=jax.ShapeDtypeStruct((cells, columns), jnp.float32),
        name="stencil",
    )(field, from_east, from_west)

    zonal_part = jnp.sum(lines[0] * sensitivity, axis=1)
    spread_out = jnp.broadcast_to(zonal_part[None], (slabs, cells))
    everyone = lax.all_to_all(spread_out, "lon", 0, 0, tiled=True)
    summed = jnp.sum(everyone, axis=0).reshape(zonal_control.shape)
    zonal_grad = zonal_control + summed * zscale

    sens = [shift(sensitivity, "lat", d) if d else sensitivity for d in (2, 1, 0, -1, -2)]
    here = pl.BlockSpec(block, lambda j, rank, reach: (j, 0, 0, 0))
    taken = pl.BlockSpec(block, lambda j, rank, reach: (jnp.minimum(rank[j], most - 1), 0, 0, 0))
    grad = pl.pallas_call(
        functools.partial(mixed_kernel, scale=scale),
        grid_spec=pltpu.PrefetchScalarGridSpec(
            num_scalar_prefetch=2,
            grid=(blocks,),
            in_specs=[fixed((cells, columns))] * 5 + [here] + [taken] * 4,
            out_specs=here,
        ),
        out_shape=jax.ShapeDtypeStruct((blocks, group, cells, columns), jnp.float32),
        name="mixed",
    )(rank, loc_reach, *sens, own, up1, down1, up2, down2)
    return grad.reshape(ens_control.shape), zonal_grad


def solution(mesh):
    return jax.shard_map(
        local,
        mesh=mesh,
        in_specs=(
            P(None, None, None, "lat", "lon"),
            P(None, None, None, "lat", "lon"),
            P(None, None, "lat"),
            P(None, None, "lat", "lon"),
            P(None, None, "lat", "lon"),
            P("lat", "lon"),
            P(None, None, None, "lat", "lon"),
            P(),
        ),
        out_specs=(P(None, None, None, "lat", "lon"), P(None, None, "lat")),
        check_vma=False,
    )
```

```python
import functools
import math

import jax
import jax.numpy as jnp
from jax import lax
from jax.experimental import pallas as pl
from jax.experimental.pallas import tpu as pltpu
from jax.sharding import PartitionSpec as P


NU = 0.2
REACH = 2
HALO = 4
PAD = 16
LANES = 128
PACK = LANES // HALO
LEAST = 3
FEW = 4
VMEM = pltpu.MemorySpace.VMEM
SMEM = pltpu.MemorySpace.SMEM


def shift(value, axis, distance):
    peers = lax.axis_size(axis)
    return lax.ppermute(value, axis, [((i - distance) % peers, i) for i in range(peers)])


def sort_kernel(reach, own, out, order, rank, case, sems):
    blocks = own.shape[0]
    for j in range(blocks):
        place = jnp.int32(0)
        for i in range(blocks):
            if i != j:
                ahead = reach[i] >= reach[j] if i < j else reach[i] > reach[j]
                place = place + ahead.astype(jnp.int32)
        rank[j] = place
        order[place] = j
        pltpu.make_async_copy(own.at[j], out.at[place], sems.at[j]).start()
    near, far = jnp.int32(0), jnp.int32(0)
    for j in range(blocks):
        near = near + (reach[j] >= 1).astype(jnp.int32)
        far = far + (reach[j] >= 2).astype(jnp.int32)
    near = jnp.maximum(near, LEAST)
    chosen = jnp.clip(far - 2, 0, FEW - 1)
    for n, first in enumerate(send_sizes(blocks - 1)[1]):
        chosen = chosen + jnp.where(near == LEAST + n, first, 0)
    case[0] = chosen
    for j in range(blocks):
        pltpu.make_async_copy(own.at[j], out.at[rank[j]], sems.at[j]).wait()


def held(*arrays):
    return [pltpu.with_memory_space_constraint(x, VMEM) for x in arrays]


def send_sizes(most):
    sizes, starts = [], []
    for near in range(LEAST, most + 1):
        starts.append(len(sizes))
        far = list(range(2, min(near, FEW) + 1))
        sizes += [(near, n) for n in far + [near] * (near > FEW)]
    return sizes, starts


def weight_of(reach, distance):
    limit = jnp.full((1, LANES), reach.astype(jnp.float32)) + 1.0
    return jnp.maximum(0.0, 1.0 - distance / limit)


def pairs_kernel(
    order, reach, zonal, own, control, up1, down1, up2, down2, prior, flow, seen, sea,
    to_up1, to_down1, to_up2, to_down2, to_up3, to_down3,
    sums, rows, own_b, control_b, up1_b, down1_b, up2_b, down2_b, sems, *, scale, zscale
):
    n = sums.shape[1]
    blocks = own.shape[0]
    always = [(own, own_b), (control, control_b)]
    near = [(up1, up1_b), (down1, down1_b)]
    far = [(up2, up2_b), (down2, down2_b)]

    def copies(i):
        found = {0: [], 1: [], 2: []}
        for k, (source, buffer) in enumerate(always + near + far):
            if i < source.shape[0]:
                at = order[i] if source is control else i
                copy = pltpu.make_async_copy(source.at[at], buffer.at[i], sems.at[k, i])
                found[k // 2].append(copy)
        return found

    for i in range(blocks):
        found = copies(i)
        for least in (0, 1, 2):
            if found[least]:

                @pl.when(reach[order[i]] >= least)
                def _(group=found[least]):
                    for copy in group:
                        copy.start()

    sums[...] = jnp.zeros(sums.shape, sums.dtype)
    levels, tall = zonal.shape[1:]
    for row in range(n):
        value = zonal[row // (levels * tall), row // tall % levels, row % tall]
        rows[row : row + 1] = jnp.full((1, LANES), value)

    for i in range(blocks):
        here = reach[order[i]]
        found = copies(i)

        def added(buffer, i=i):
            total = None
            for m in range(control.shape[1]):
                term = buffer[i, m].astype(jnp.float32) * control_b[i, m].astype(jnp.float32)
                total = term if total is None else total + term
            return total

        for copy in found[0]:
            copy.wait()
        sums[2] += weight_of(here, 0.0) * added(own_b)
        for least, up, down in ((1, up1_b, down1_b), (2, up2_b, down2_b)):
            if found[least]:

                @pl.when(here >= least)
                def _(least=least, up=up, down=down, here=here, group=found[least], added=added):
                    for copy in group:
                        copy.wait()
                    w = weight_of(here, float(least))
                    sums[2 + least] += w * added(up)
                    sums[2 - least] += w * added(down)

    part = [sums[o] * scale for o in range(5)]
    part[2] = part[2] + prior[...] * rows[...] * zscale
    for k in range(3):
        to_up1[k * n : (k + 1) * n] = part[2 + k]
        to_down1[k * n : (k + 1) * n] = part[k]
    for k in range(2):
        to_up2[k * n : (k + 1) * n] = part[3 + k]
        to_down2[k * n : (k + 1) * n] = part[k]
    to_up3[...] = part[4]
    to_down3[...] = part[0]
    for out in (to_up1, to_down1):
        at = 3 * n
        for source in (flow, seen):
            out[at : at + source.shape[0]] = source[...]
            at += source.shape[0]
        out[at : at + sea.shape[0]] = sea[...].astype(jnp.float32)


def mixed_kernel(
    rank, reach, down2_s, down1_s, own_s, up1_s, up2_s, own, up1, down1, up2, down2,
    out, own_b, up1_b, down1_b, up2_b, down2_b, out_b, sems, *, scale
):
    blocks = own.shape[0]
    pieces = [
        [(own, own_b, own_s)],
        [(up1, up1_b, up1_s), (down1, down1_b, down1_s)],
        [(up2, up2_b, up2_s), (down2, down2_b, down2_s)],
    ]

    def copies(j, d):
        found = []
        for k, (source, buffer, _) in enumerate(pieces[d]):
            at = j if d == 0 else jnp.minimum(rank[j], source.shape[0] - 1)
            sem = sems.at[max(0, 2 * d - 1) + k, j]
            found.append(pltpu.make_async_copy(source.at[at], buffer.at[j], sem))
        return found

    def written(j):
        return pltpu.make_async_copy(out_b.at[j], out.at[j], sems.at[5, j])

    for j in range(blocks):
        for d in range(REACH + 1):

            @pl.when(reach[j] >= d)
            def _(j=j, d=d):
                for copy in copies(j, d):
                    copy.start()

    def run(j, last):
        weights = [weight_of(reach[j], float(d)) for d in range(last + 1)]
        for d in range(last + 1):
            for copy in copies(j, d):
                copy.wait()
        scaled = [[sens[...] * scale for _, _, sens in pieces[d]] for d in range(last + 1)]
        for m in range(own.shape[1]):
            total = None
            for d in range(last + 1):
                near = None
                for (_, buffer, _), sens in zip(pieces[d], scaled[d]):
                    value = buffer[j, m].astype(jnp.float32) * sens
                    value = value.astype(jnp.bfloat16).astype(jnp.float32)
                    near = value if near is None else near + value
                near = weights[d] * near
                total = near if total is None else total + near
            out_b[j, m] = total

    def step(j, carry):
        for d in range(REACH + 1):
            here = reach[j]
            pl.when(here >= d if d == REACH else here == d)(lambda d=d: run(j, d))
        written(j).start()
        return carry

    lax.fori_loop(0, blocks, step, 0)
    for j in range(blocks):
        written(j).wait()


def lane(shape):
    return lax.broadcasted_iota(jnp.int32, shape, len(shape) - 1)


def gather_kernel(inside, up, down, r1, m1, r2, m2, r3, m3, field, west_edge, east_edge):
    n = r3.shape[0]
    low, high = inside[0] > 0, inside[1] > 0
    south = down[n : 2 * n] + r1[:n] + m1[:n] + r2[:n] + r3[...]
    mid = up[:n] + r1[n : 2 * n] + m1[n : 2 * n] + r2[n : 2 * n] + m2[:n]
    north = up[n : 2 * n] + r1[2 * n : 3 * n] + m1[2 * n : 3 * n] + m2[n : 2 * n] + m3[...]
    field[:, 12:PAD] = jnp.zeros((field.shape[0], PAD - 12, LANES), jnp.float32)
    south, north = jnp.where(low, south, 0.0), jnp.where(high, north, 0.0)
    for i in range(n // 4):
        field[i, 0:4] = south[4 * i : 4 * i + 4]
        field[i, 4:8] = mid[4 * i : 4 * i + 4]
        field[i, 8:12] = north[4 * i : 4 * i + 4]
    for i in range(n // 4, field.shape[0]):
        at = pl.ds(2 * n + 4 * i, 4)
        field[i, 0:4] = jnp.where(low, r1[at], 0.0)
        field[i, 4:8] = up[at]
        field[i, 8:12] = jnp.where(high, m1[at], 0.0)
    spot = lane((PAD, LANES)) // HALO
    for g in range(west_edge.shape[0]):
        west = jnp.zeros((PAD, LANES), jnp.float32)
        east = jnp.zeros((PAD, LANES), jnp.float32)
        for k in range(min(PACK, field.shape[0] - g * PACK)):
            value = field[g * PACK + k]
            at = HALO * k
            west = jnp.where(spot == k, pltpu.roll(value, at, 1) if at else value, west)
            east = jnp.where(spot == k, pltpu.roll(value, (at + HALO) % LANES, 1) if at + HALO < LANES else value, east)
        west_edge[g] = west
        east_edge[g] = east


def stencil_kernel(field, from_east, from_west, spread, out, zonal):
    n = out.shape[0] // 4
    cols = lane((PAD, LANES))

    def turn(value, amount):
        return pltpu.roll(value, amount % LANES, 1) if amount % LANES else value

    def wide(i):
        g, at = i // PACK, HALO * (i % PACK)
        right = turn(from_east[g], -at)
        left = turn(from_west[g], -at - HALO)
        beside = jnp.where(cols < HALO, right, jnp.where(cols >= LANES - HALO, left, 0.0))
        return field[i], beside

    def at_west(v):
        a, b = pltpu.roll(v[0], 1, 1), pltpu.roll(v[1], 1, 1)
        return jnp.where(cols == 0, b, a), jnp.where(cols == 0, a, b)

    def at_east(v):
        a, b = pltpu.roll(v[0], LANES - 1, 1), pltpu.roll(v[1], LANES - 1, 1)
        return jnp.where(cols == LANES - 1, b, a), jnp.where(cols == LANES - 1, a, b)

    def at_north(v):
        return tuple(pltpu.roll(x, PAD - 1, 0) for x in v)

    def at_south(v):
        return tuple(pltpu.roll(x, 1, 0) for x in v)

    def each(f, *vs):
        return tuple(f(*xs) for xs in zip(*vs))

    def mul(a, b):
        return each(lambda x, y: x * y, a, b)

    def sub(a, b):
        return each(lambda x, y: x - y, a, b)

    def total(*vs):
        return each(lambda *xs: sum(xs[1:], xs[0]), *vs)

    centre = 1.0 - 4.0 * NU
    levels = n // 3
    sea = wide(field.shape[0] - 1)
    for l in range(levels):
        cu, cv = wide(n + l), wide(n + levels + l)
        east_c = each(lambda x: NU - 0.5 * x, cu)
        west_c = each(lambda x: NU + 0.5 * x, cu)
        north_c = each(lambda x: NU - 0.5 * x, cv)
        south_c = each(lambda x: NU + 0.5 * x, cv)

        def tangent(f):
            return mul(
                sea,
                total(
                    each(lambda x: centre * x, f),
                    mul(east_c, at_east(f)),
                    mul(west_c, at_west(f)),
                    mul(north_c, at_north(f)),
                    mul(south_c, at_south(f)),
                ),
            )

        def adjoint(f):
            z = mul(sea, f)
            return total(
                each(lambda x: centre * x, z),
                at_west(mul(east_c, z)),
                at_east(mul(west_c, z)),
                at_south(mul(north_c, z)),
                at_north(mul(south_c, z)),
            )

        for t in range(3):
            i = t * levels + l
            first = tangent(wide(i))
            second = tangent(first)
            near = wide(n + 2 * levels + i)
            later = wide(n + 2 * levels + n + i)
            weighted = total(sub(first, near), adjoint(sub(second, later)))
            out[4 * i : 4 * i + 4] = adjoint(weighted)[0][4:8]
    zonal[...] = lax.dot_general(
        jnp.ones((zonal.shape[0], LANES), jnp.float32),
        out[...] * spread[...],
        (((1,), (1,)), ((), ())),
        precision=lax.Precision.HIGHEST,
        preferred_element_type=jnp.float32,
    )


def whole():
    return pl.BlockSpec(memory_space=VMEM)


def local(
    ens_control, perturbations, zonal_control, spread, currents, sea_mask, observed, loc_reach
):
    bands = lax.axis_size("lat")
    slabs = lax.axis_size("lon")
    members, tracers, levels, rows, columns = ens_control.shape
    blocks = loc_reach.shape[0]
    group = members // blocks
    cells = tracers * levels * rows
    scale = 1.0 / math.sqrt(members - 1)
    zscale = 1.0 / math.sqrt(columns * slabs)
    own = perturbations.reshape(blocks, group, cells, columns)
    control = ens_control.reshape(blocks, group, cells, columns)
    most = blocks - 1
    place = pl.BlockSpec(memory_space=pl.ANY)
    small = pl.BlockSpec(memory_space=SMEM)
    sending, order, rank, case = pl.pallas_call(
        sort_kernel,
        in_specs=[small, place],
        out_specs=[place, small, small, small],
        out_shape=[
            jax.ShapeDtypeStruct(own.shape, own.dtype),
            jax.ShapeDtypeStruct((blocks,), jnp.int32),
            jax.ShapeDtypeStruct((blocks,), jnp.int32),
            jax.ShapeDtypeStruct((1,), jnp.int32),
        ],
        scratch_shapes=[pltpu.SemaphoreType.DMA((blocks,))],
        name="sort",
    )(loc_reach, own)

    def exchange(near, far):
        def run(block):
            got = []
            for distance, n in ((-1, near), (1, near), (-2, far), (2, far)):
                moved = shift(block[:n], "lat", distance)
                rest = jnp.zeros((most - n,) + block.shape[1:], block.dtype)
                got.append(jnp.concatenate([moved, rest], axis=0) if n < most else moved)
            return tuple(got)

        return run

    cases = [exchange(near, far) for near, far in send_sizes(most)[0]]
    up1, down1, up2, down2 = lax.optimization_barrier(lax.switch(case[0], cases, sending))

    items = tracers * levels
    lines = [x.reshape(-1, columns) for x in (spread, currents, observed, sea_mask)]
    beside = sum(x.shape[0] for x in lines[1:])
    messages = [3 * cells + beside] * 2 + [2 * cells] * 2 + [cells] * 2

    def buffers(*counts):
        return [pltpu.VMEM((n, group, cells, columns), own.dtype) for n in counts]

    to_up1, to_down1, to_up2, to_down2, to_up3, to_down3 = pl.pallas_call(
        functools.partial(pairs_kernel, scale=scale, zscale=zscale),
        in_specs=[small] * 3 + [place] * 6 + [whole()] * 4,
        out_specs=[whole()] * 6,
        scratch_shapes=[
            pltpu.VMEM((5, cells, columns), jnp.float32),
            pltpu.VMEM((cells, columns), jnp.float32),
            *buffers(blocks, blocks, most, most, most, most),
            pltpu.SemaphoreType.DMA((6, blocks)),
        ],
        out_shape=[pltpu.VMEM((n, columns), jnp.float32) for n in messages],
        name="pairs",
    )(order, loc_reach, zonal_control, sending, control, up1, down1, up2, down2, *lines)

    r1, m1 = shift(to_up1, "lat", 1), shift(to_down1, "lat", -1)
    r2, m2 = shift(to_up2, "lat", 2), shift(to_down2, "lat", -2)
    r3, m3 = shift(to_up3, "lat", 3), shift(to_down3, "lat", -3)
    band = lax.axis_index("lat")
    inside = jnp.stack([band > 0, band < bands - 1]).astype(jnp.int32)
    total = items + beside // rows
    packs = -(-total // PACK)
    field, west_edge, east_edge = pl.pallas_call(
        gather_kernel,
        in_specs=[small] + [whole()] * 8,
        out_specs=[whole()] * 3,
        out_shape=[
            pltpu.VMEM((total, PAD, columns), jnp.float32),
            pltpu.VMEM((packs, PAD, columns), jnp.float32),
            pltpu.VMEM((packs, PAD, columns), jnp.float32),
        ],
        name="gather",
    )(inside, *held(to_up1, to_down1, r1, m1, r2, m2, r3, m3))
    from_east = shift(west_edge, "lon", -1)
    from_west = shift(east_edge, "lon", 1)
    sensitivity, zonal_part = pl.pallas_call(
        stencil_kernel,
        in_specs=[whole()] * 4,
        out_specs=[whole()] * 2,
        out_shape=[
            pltpu.VMEM((cells, columns), jnp.float32),
            jax.ShapeDtypeStruct((slabs, cells), jnp.float32),
        ],
        name="stencil",
    )(*held(field, from_east, from_west), lines[0])

    everyone = lax.all_to_all(zonal_part, "lon", 0, 0, tiled=True)
    summed = jnp.sum(everyone, axis=0).reshape(zonal_control.shape)
    zonal_grad = zonal_control + summed * zscale

    sens = [shift(sensitivity, "lat", d) if d else sensitivity for d in (2, 1, 0, -1, -2)]
    grad = pl.pallas_call(
        functools.partial(mixed_kernel, scale=scale),
        in_specs=[small] * 2 + [whole()] * 5 + [place] * 5,
        out_specs=place,
        scratch_shapes=[
            *buffers(*[blocks] * 5),
            pltpu.VMEM((blocks, group, cells, columns), jnp.float32),
            pltpu.SemaphoreType.DMA((6, blocks)),
        ],
        out_shape=jax.ShapeDtypeStruct((blocks, group, cells, columns), jnp.float32),
        name="mixed",
    )(rank, loc_reach, *held(*sens), own, up1, down1, up2, down2)
    return grad.reshape(ens_control.shape), zonal_grad


def solution(mesh):
    return jax.shard_map(
        local,
        mesh=mesh,
        in_specs=(
            P(None, None, None, "lat", "lon"),
            P(None, None, None, "lat", "lon"),
            P(None, None, "lat"),
            P(None, None, "lat", "lon"),
            P(None, None, "lat", "lon"),
            P("lat", "lon"),
            P(None, None, None, "lat", "lon"),
            P(),
        ),
        out_specs=(P(None, None, None, "lat", "lon"), P(None, None, "lat")),
        check_vma=False,
    )
```

```python
import functools
import math

import jax
import jax.numpy as jnp
from jax import lax
from jax.experimental import pallas as pl
from jax.experimental.pallas import tpu as pltpu
from jax.sharding import PartitionSpec as P


NU = 0.2
REACH = 2
HALO = 4
PAD = 16
LANES = 128
PACK = LANES // HALO
ROW = 4
LEAST = 4
FEW = 4
VMEM = pltpu.MemorySpace.VMEM
SMEM = pltpu.MemorySpace.SMEM


def shift(value, axis, distance):
    peers = lax.axis_size(axis)
    return lax.ppermute(value, axis, [((i - distance) % peers, i) for i in range(peers)])


def sort_kernel(reach, own, out, order, rank, case, sems):
    blocks = own.shape[0]
    for j in range(blocks):
        place = jnp.int32(0)
        for i in range(blocks):
            if i != j:
                ahead = reach[i] >= reach[j] if i < j else reach[i] > reach[j]
                place = place + ahead.astype(jnp.int32)
        rank[j] = place
        order[place] = j
        pltpu.make_async_copy(own.at[j], out.at[place], sems.at[j]).start()
    near, far = jnp.int32(0), jnp.int32(0)
    for j in range(blocks):
        near = near + (reach[j] >= 1).astype(jnp.int32)
        far = far + (reach[j] >= 2).astype(jnp.int32)
    near = jnp.maximum(near, LEAST)
    chosen, first = jnp.int32(0), 0
    for n, sizes in send_sizes(blocks - 1).items():
        spot = first + sum((far > size).astype(jnp.int32) for size in sizes[:-1])
        chosen = jnp.where(near == n, spot, chosen)
        first += len(sizes)
    case[0] = chosen
    for j in range(blocks):
        pltpu.make_async_copy(own.at[j], out.at[rank[j]], sems.at[j]).wait()


def place_kernel(inner_up, inner_down, direct, relayed, far_up, far_down, up1, down1, up2, down2, sems):
    spot = lax.axis_index("lat") % ROW

    def copies(out, *sources):
        found, at = [], 0
        for source in sources:
            n = source.shape[0]
            slot = sems.at[len(started), len(found)]
            found.append(pltpu.make_async_copy(source, out.at[pl.ds(at, n)], slot))
            at += n
        started.append(found)
        return found

    started = []
    cases = [
        (spot == ROW - 1, copies(up1, direct, relayed)),
        (spot != ROW - 1, copies(up1, inner_up)),
        (spot == 0, copies(down1, direct, relayed)),
        (spot != 0, copies(down1, inner_down)),
        (spot >= 0, copies(up2, far_up)),
        (spot >= 0, copies(down2, far_down)),
    ]
    for taken, group in cases:

        @pl.when(taken)
        def _(group=group):
            for copy in group:
                copy.start()

    for taken, group in cases:

        @pl.when(taken)
        def _(group=group):
            for copy in group:
                copy.wait()


def held(*arrays):
    return [pltpu.with_memory_space_constraint(x, VMEM) for x in arrays]


def send_sizes(most):
    sizes = {}
    for near in range(LEAST, most + 1):
        sizes[near] = [n for n in range(2, FEW + 1) if n < near] + [near]
    sizes[most] = [FEW, most]
    return sizes


def weight_of(reach, distance):
    limit = jnp.full((1, LANES), reach.astype(jnp.float32)) + 1.0
    return jnp.maximum(0.0, 1.0 - distance / limit)


def pairs_kernel(
    order, reach, zonal, own, control, up1, down1, up2, down2, prior, flow, seen, sea,
    to_up1, to_down1, to_up2, to_down2, to_up3, to_down3,
    sums, rows, own_b, control_b, up1_b, down1_b, up2_b, down2_b, sems, *, scale, zscale
):
    n = sums.shape[1]
    blocks = own.shape[0]
    always = [(own, own_b), (control, control_b)]
    near = [(up1, up1_b), (down1, down1_b)]
    far = [(up2, up2_b), (down2, down2_b)]

    def copies(i):
        found = {0: [], 1: [], 2: []}
        for k, (source, buffer) in enumerate(always + near + far):
            if i < source.shape[0]:
                at = order[i] if source is control else i
                copy = pltpu.make_async_copy(source.at[at], buffer.at[i], sems.at[k, i])
                found[k // 2].append(copy)
        return found

    for i in range(blocks):
        found = copies(i)
        for least in (0, 1, 2):
            if found[least]:

                @pl.when(reach[order[i]] >= least)
                def _(group=found[least]):
                    for copy in group:
                        copy.start()

    sums[...] = jnp.zeros(sums.shape, sums.dtype)
    levels, tall = zonal.shape[1:]
    for row in range(n):
        value = zonal[row // (levels * tall), row // tall % levels, row % tall]
        rows[row : row + 1] = jnp.full((1, LANES), value)

    for i in range(blocks):
        here = reach[order[i]]
        found = copies(i)

        def added(buffer, i=i):
            total = None
            for m in range(control.shape[1]):
                term = buffer[i, m].astype(jnp.float32) * control_b[i, m].astype(jnp.float32)
                total = term if total is None else total + term
            return total

        for copy in found[0]:
            copy.wait()
        sums[2] += weight_of(here, 0.0) * added(own_b)
        for least, up, down in ((1, up1_b, down1_b), (2, up2_b, down2_b)):
            if found[least]:

                @pl.when(here >= least)
                def _(least=least, up=up, down=down, here=here, group=found[least], added=added):
                    for copy in group:
                        copy.wait()
                    w = weight_of(here, float(least))
                    sums[2 + least] += w * added(up)
                    sums[2 - least] += w * added(down)

    part = [sums[o] * scale for o in range(5)]
    part[2] = part[2] + prior[...] * rows[...] * zscale
    for k in range(3):
        to_up1[k * n : (k + 1) * n] = part[2 + k]
        to_down1[k * n : (k + 1) * n] = part[k]
    for k in range(2):
        to_up2[k * n : (k + 1) * n] = part[3 + k]
        to_down2[k * n : (k + 1) * n] = part[k]
    to_up3[...] = part[4]
    to_down3[...] = part[0]
    for out in (to_up1, to_down1):
        at = 3 * n
        for source in (flow, seen):
            out[at : at + source.shape[0]] = source[...]
            at += source.shape[0]
        out[at : at + sea.shape[0]] = sea[...].astype(jnp.float32)


def mixed_kernel(
    rank, reach, down2_s, down1_s, own_s, up1_s, up2_s, own, up1, down1, up2, down2,
    out, own_b, up1_b, down1_b, up2_b, down2_b, out_b, sems, *, scale
):
    blocks = own.shape[0]
    pieces = [
        [(own, own_b, own_s)],
        [(up1, up1_b, up1_s), (down1, down1_b, down1_s)],
        [(up2, up2_b, up2_s), (down2, down2_b, down2_s)],
    ]

    def copies(j, d):
        found = []
        for k, (source, buffer, _) in enumerate(pieces[d]):
            at = j if d == 0 else jnp.minimum(rank[j], source.shape[0] - 1)
            sem = sems.at[max(0, 2 * d - 1) + k, j]
            found.append(pltpu.make_async_copy(source.at[at], buffer.at[j], sem))
        return found

    def written(j):
        return pltpu.make_async_copy(out_b.at[j], out.at[j], sems.at[5, j])

    for j in range(blocks):
        for d in range(REACH + 1):

            @pl.when(reach[j] >= d)
            def _(j=j, d=d):
                for copy in copies(j, d):
                    copy.start()

    def run(j, last):
        weights = [weight_of(reach[j], float(d)) for d in range(last + 1)]
        for d in range(last + 1):
            for copy in copies(j, d):
                copy.wait()
        scaled = [[sens[...] * scale for _, _, sens in pieces[d]] for d in range(last + 1)]
        for m in range(own.shape[1]):
            total = None
            for d in range(last + 1):
                near = None
                for (_, buffer, _), sens in zip(pieces[d], scaled[d]):
                    value = buffer[j, m].astype(jnp.float32) * sens
                    value = value.astype(jnp.bfloat16).astype(jnp.float32)
                    near = value if near is None else near + value
                near = weights[d] * near
                total = near if total is None else total + near
            out_b[j, m] = total

    def step(j, carry):
        for d in range(REACH + 1):
            here = reach[j]
            pl.when(here >= d if d == REACH else here == d)(lambda d=d: run(j, d))
        written(j).start()
        return carry

    lax.fori_loop(0, blocks, step, 0)
    for j in range(blocks):
        written(j).wait()


def lane(shape):
    return lax.broadcasted_iota(jnp.int32, shape, len(shape) - 1)


def gather_kernel(up, down, r1, m1, r2, m2, r3, m3, field, west_edge, east_edge):
    n = r3.shape[0]
    band = lax.axis_index("lat")
    low, high = band > 0, band < lax.axis_size("lat") - 1
    south = down[n : 2 * n] + r1[:n] + m1[:n] + r2[:n] + r3[...]
    mid = up[:n] + r1[n : 2 * n] + m1[n : 2 * n] + r2[n : 2 * n] + m2[:n]
    north = up[n : 2 * n] + r1[2 * n : 3 * n] + m1[2 * n : 3 * n] + m2[n : 2 * n] + m3[...]
    field[:, 12:PAD] = jnp.zeros((field.shape[0], PAD - 12, LANES), jnp.float32)
    south, north = jnp.where(low, south, 0.0), jnp.where(high, north, 0.0)
    for i in range(n // 4):
        field[i, 0:4] = south[4 * i : 4 * i + 4]
        field[i, 4:8] = mid[4 * i : 4 * i + 4]
        field[i, 8:12] = north[4 * i : 4 * i + 4]
    for i in range(n // 4, field.shape[0]):
        at = pl.ds(2 * n + 4 * i, 4)
        field[i, 0:4] = jnp.where(low, r1[at], 0.0)
        field[i, 4:8] = up[at]
        field[i, 8:12] = jnp.where(high, m1[at], 0.0)
    spot = lane((PAD, LANES)) // HALO
    for g in range(west_edge.shape[0]):
        west = jnp.zeros((PAD, LANES), jnp.float32)
        east = jnp.zeros((PAD, LANES), jnp.float32)
        for k in range(min(PACK, field.shape[0] - g * PACK)):
            value = field[g * PACK + k]
            at = HALO * k
            west = jnp.where(spot == k, pltpu.roll(value, at, 1) if at else value, west)
            east = jnp.where(spot == k, pltpu.roll(value, (at + HALO) % LANES, 1) if at + HALO < LANES else value, east)
        west_edge[g] = west
        east_edge[g] = east


def stencil_kernel(field, from_east, from_west, spread, out, zonal):
    n = out.shape[0] // 4
    cols = lane((PAD, LANES))

    def turn(value, amount):
        return pltpu.roll(value, amount % LANES, 1) if amount % LANES else value

    def wide(i):
        g, at = i // PACK, HALO * (i % PACK)
        right = turn(from_east[g], -at)
        left = turn(from_west[g], -at - HALO)
        beside = jnp.where(cols < HALO, right, jnp.where(cols >= LANES - HALO, left, 0.0))
        return field[i], beside

    def at_west(v):
        a, b = pltpu.roll(v[0], 1, 1), pltpu.roll(v[1], 1, 1)
        return jnp.where(cols == 0, b, a), jnp.where(cols == 0, a, b)

    def at_east(v):
        a, b = pltpu.roll(v[0], LANES - 1, 1), pltpu.roll(v[1], LANES - 1, 1)
        return jnp.where(cols == LANES - 1, b, a), jnp.where(cols == LANES - 1, a, b)

    def at_north(v):
        return tuple(pltpu.roll(x, PAD - 1, 0) for x in v)

    def at_south(v):
        return tuple(pltpu.roll(x, 1, 0) for x in v)

    def each(f, *vs):
        return tuple(f(*xs) for xs in zip(*vs))

    def mul(a, b):
        return each(lambda x, y: x * y, a, b)

    def sub(a, b):
        return each(lambda x, y: x - y, a, b)

    def total(*vs):
        return each(lambda *xs: sum(xs[1:], xs[0]), *vs)

    centre = 1.0 - 4.0 * NU
    levels = n // 3
    sea = wide(field.shape[0] - 1)
    for l in range(levels):
        cu, cv = wide(n + l), wide(n + levels + l)
        east_c = each(lambda x: NU - 0.5 * x, cu)
        west_c = each(lambda x: NU + 0.5 * x, cu)
        north_c = each(lambda x: NU - 0.5 * x, cv)
        south_c = each(lambda x: NU + 0.5 * x, cv)

        def tangent(f):
            return mul(
                sea,
                total(
                    each(lambda x: centre * x, f),
                    mul(east_c, at_east(f)),
                    mul(west_c, at_west(f)),
                    mul(north_c, at_north(f)),
                    mul(south_c, at_south(f)),
                ),
            )

        def adjoint(f):
            z = mul(sea, f)
            return total(
                each(lambda x: centre * x, z),
                at_west(mul(east_c, z)),
                at_east(mul(west_c, z)),
                at_south(mul(north_c, z)),
                at_north(mul(south_c, z)),
            )

        for t in range(3):
            i = t * levels + l
            first = tangent(wide(i))
            second = tangent(first)
            near = wide(n + 2 * levels + i)
            later = wide(n + 2 * levels + n + i)
            weighted = total(sub(first, near), adjoint(sub(second, later)))
            out[4 * i : 4 * i + 4] = adjoint(weighted)[0][4:8]
    zonal[...] = lax.dot_general(
        jnp.ones((zonal.shape[0], LANES), jnp.float32),
        out[...] * spread[...],
        (((1,), (1,)), ((), ())),
        precision=lax.Precision.HIGHEST,
        preferred_element_type=jnp.float32,
    )


def whole():
    return pl.BlockSpec(memory_space=VMEM)


def local(
    ens_control, perturbations, zonal_control, spread, currents, sea_mask, observed, loc_reach
):
    bands = lax.axis_size("lat")
    slabs = lax.axis_size("lon")
    members, tracers, levels, rows, columns = ens_control.shape
    blocks = loc_reach.shape[0]
    group = members // blocks
    cells = tracers * levels * rows
    scale = 1.0 / math.sqrt(members - 1)
    zscale = 1.0 / math.sqrt(columns * slabs)
    own = perturbations.reshape(blocks, group, cells, columns)
    control = ens_control.reshape(blocks, group, cells, columns)
    most = blocks - 1
    place = pl.BlockSpec(memory_space=pl.ANY)
    small = pl.BlockSpec(memory_space=SMEM)
    sending, order, rank, case = pl.pallas_call(
        sort_kernel,
        in_specs=[small, place],
        out_specs=[place, small, small, small],
        out_shape=[
            jax.ShapeDtypeStruct(own.shape, own.dtype),
            jax.ShapeDtypeStruct((blocks,), jnp.int32),
            jax.ShapeDtypeStruct((blocks,), jnp.int32),
            jax.ShapeDtypeStruct((1,), jnp.int32),
        ],
        scratch_shapes=[pltpu.SemaphoreType.DMA((blocks,))],
        name="sort",
    )(loc_reach, own)

    inner_on = [(b, b + 1) for b in range(bands) if b % ROW != ROW - 1]
    inner_back = [(b, b - 1) for b in range(bands) if b % ROW]
    firsts, lasts = range(0, bands, ROW), range(ROW - 1, bands, ROW)
    ends = [(b, (b + 1) % bands) for b in lasts] + [(b, (b - 1) % bands) for b in firsts]
    turns = [(b, b - ROW + 1) for b in lasts] + [(b, b + ROW - 1) for b in firsts]
    hops = [(b, (b + ROW) % bands) for b in firsts] + [(b, (b - ROW) % bands) for b in lasts]

    def exchange(near, far):
        def run(block):
            relay = near // 2
            bent = lax.ppermute(block[near - relay : near], "lat", turns)
            direct = lax.ppermute(block[: near - relay], "lat", ends)
            inner_up = lax.ppermute(block[:near], "lat", inner_back)
            inner_down = lax.ppermute(block[:near], "lat", inner_on)
            far_up, far_down = shift(block[:far], "lat", -2), shift(block[:far], "lat", 2)
            relayed = lax.ppermute(bent, "lat", hops)
            return tuple(
                pl.pallas_call(
                    place_kernel,
                    in_specs=[whole()] * 6,
                    out_specs=[place] * 4,
                    out_shape=[jax.ShapeDtypeStruct((most,) + block.shape[1:], block.dtype)] * 4,
                    scratch_shapes=[pltpu.SemaphoreType.DMA((6, 2))],
                    name="place",
                )(*held(inner_up, inner_down, direct, relayed, far_up, far_down))
            )

        return run

    sizes = send_sizes(most)
    cases = [exchange(near, far) for near in sizes for far in sizes[near]]
    up1, down1, up2, down2 = lax.optimization_barrier(lax.switch(case[0], cases, sending))

    items = tracers * levels
    lines = [x.reshape(-1, columns) for x in (spread, currents, observed, sea_mask)]
    beside = sum(x.shape[0] for x in lines[1:])
    messages = [3 * cells + beside] * 2 + [2 * cells] * 2 + [cells] * 2

    def buffers(*counts):
        return [pltpu.VMEM((n, group, cells, columns), own.dtype) for n in counts]

    to_up1, to_down1, to_up2, to_down2, to_up3, to_down3 = pl.pallas_call(
        functools.partial(pairs_kernel, scale=scale, zscale=zscale),
        in_specs=[small] * 3 + [place] * 6 + [whole()] * 4,
        out_specs=[whole()] * 6,
        scratch_shapes=[
            pltpu.VMEM((5, cells, columns), jnp.float32),
            pltpu.VMEM((cells, columns), jnp.float32),
            *buffers(blocks, blocks, most, most, most, most),
            pltpu.SemaphoreType.DMA((6, blocks)),
        ],
        out_shape=[pltpu.VMEM((n, columns), jnp.float32) for n in messages],
        name="pairs",
    )(order, loc_reach, zonal_control, sending, control, up1, down1, up2, down2, *lines)

    r1, m1 = shift(to_up1, "lat", 1), shift(to_down1, "lat", -1)
    r2, m2 = shift(to_up2, "lat", 2), shift(to_down2, "lat", -2)
    r3, m3 = shift(to_up3, "lat", 3), shift(to_down3, "lat", -3)
    total = items + beside // rows
    packs = -(-total // PACK)
    field, west_edge, east_edge = pl.pallas_call(
        gather_kernel,
        in_specs=[whole()] * 8,
        out_specs=[whole()] * 3,
        out_shape=[
            pltpu.VMEM((total, PAD, columns), jnp.float32),
            pltpu.VMEM((packs, PAD, columns), jnp.float32),
            pltpu.VMEM((packs, PAD, columns), jnp.float32),
        ],
        name="gather",
    )(*held(to_up1, to_down1, r1, m1, r2, m2, r3, m3))
    from_east = shift(west_edge, "lon", -1)
    from_west = shift(east_edge, "lon", 1)
    sensitivity, zonal_part = pl.pallas_call(
        stencil_kernel,
        in_specs=[whole()] * 4,
        out_specs=[whole()] * 2,
        out_shape=[
            pltpu.VMEM((cells, columns), jnp.float32),
            jax.ShapeDtypeStruct((slabs, cells), jnp.float32),
        ],
        name="stencil",
    )(*held(field, from_east, from_west), lines[0])

    everyone = lax.all_to_all(zonal_part, "lon", 0, 0, tiled=True)
    summed = jnp.sum(everyone, axis=0).reshape(zonal_control.shape)
    zonal_grad = zonal_control + summed * zscale

    sens = [shift(sensitivity, "lat", d) if d else sensitivity for d in (2, 1, 0, -1, -2)]
    grad = pl.pallas_call(
        functools.partial(mixed_kernel, scale=scale),
        in_specs=[small] * 2 + [whole()] * 5 + [place] * 5,
        out_specs=place,
        scratch_shapes=[
            *buffers(*[blocks] * 5),
            pltpu.VMEM((blocks, group, cells, columns), jnp.float32),
            pltpu.SemaphoreType.DMA((6, blocks)),
        ],
        out_shape=jax.ShapeDtypeStruct((blocks, group, cells, columns), jnp.float32),
        name="mixed",
    )(rank, loc_reach, *held(*sens), own, up1, down1, up2, down2)
    return grad.reshape(ens_control.shape), zonal_grad


def solution(mesh):
    return jax.shard_map(
        local,
        mesh=mesh,
        in_specs=(
            P(None, None, None, "lat", "lon"),
            P(None, None, None, "lat", "lon"),
            P(None, None, "lat"),
            P(None, None, "lat", "lon"),
            P(None, None, "lat", "lon"),
            P("lat", "lon"),
            P(None, None, None, "lat", "lon"),
            P(),
        ),
        out_specs=(P(None, None, None, "lat", "lon"), P(None, None, "lat")),
        check_vma=False,
    )
```

```python
import functools
import math

import jax
import jax.numpy as jnp
from jax import lax
from jax.experimental import pallas as pl
from jax.experimental.pallas import tpu as pltpu
from jax.sharding import PartitionSpec as P


NU = 0.2
REACH = 2
HALO = 4
PAD = 16
LANES = 128
PACK = LANES // HALO
ROW = 4
LEAST = 4
FEW = 4
VMEM = pltpu.MemorySpace.VMEM
SMEM = pltpu.MemorySpace.SMEM


def shift(value, axis, distance):
    peers = lax.axis_size(axis)
    return lax.ppermute(value, axis, [((i - distance) % peers, i) for i in range(peers)])


def sort_kernel(reach, own, out, order, rank, case, passing, sems):
    blocks = own.shape[0]
    for j in range(blocks):
        place = jnp.int32(0)
        for i in range(blocks):
            if i != j:
                ahead = reach[i] >= reach[j] if i < j else reach[i] > reach[j]
                place = place + ahead.astype(jnp.int32)
        rank[j] = place
        order[place] = j
        pltpu.make_async_copy(own.at[j], passing.at[place], sems.at[0, j]).start()
    near, far = jnp.int32(0), jnp.int32(0)
    for j in range(blocks):
        near = near + (reach[j] >= 1).astype(jnp.int32)
        far = far + (reach[j] >= 2).astype(jnp.int32)
    near = jnp.maximum(near, LEAST)
    chosen, first = jnp.int32(0), 0
    for n, sizes in send_sizes(blocks - 1).items():
        spot = first + sum((far > size).astype(jnp.int32) for size in sizes[:-1])
        chosen = jnp.where(near == n, spot, chosen)
        first += len(sizes)
    case[0] = chosen
    for j in range(blocks):
        pltpu.make_async_copy(own.at[j], passing.at[rank[j]], sems.at[0, j]).wait()
        pltpu.make_async_copy(passing.at[rank[j]], out.at[rank[j]], sems.at[1, j]).start()
    for j in range(blocks):
        pltpu.make_async_copy(passing.at[rank[j]], out.at[rank[j]], sems.at[1, j]).wait()


def place_kernel(inner_up, inner_down, direct, relayed, far_up, far_down, up1, down1, up2, down2, sems):
    spot = lax.axis_index("lat") % ROW

    def copies(out, *sources):
        found, at = [], 0
        for source in sources:
            n = source.shape[0]
            slot = sems.at[len(started), len(found)]
            found.append(pltpu.make_async_copy(source, out.at[pl.ds(at, n)], slot))
            at += n
        started.append(found)
        return found

    started = []
    cases = [
        (spot == ROW - 1, copies(up1, direct, relayed)),
        (spot != ROW - 1, copies(up1, inner_up)),
        (spot == 0, copies(down1, direct, relayed)),
        (spot != 0, copies(down1, inner_down)),
        (spot >= 0, copies(up2, far_up)),
        (spot >= 0, copies(down2, far_down)),
    ]
    for taken, group in cases:

        @pl.when(taken)
        def _(group=group):
            for copy in group:
                copy.start()

    for taken, group in cases:

        @pl.when(taken)
        def _(group=group):
            for copy in group:
                copy.wait()


def held(*arrays):
    return [pltpu.with_memory_space_constraint(x, VMEM) for x in arrays]


def send_sizes(most):
    sizes = {}
    for near in range(LEAST, most + 1):
        sizes[near] = [n for n in range(2, FEW + 1) if n < near] + [near]
    sizes[most] = [FEW, most]
    return sizes


def weight_of(reach, distance):
    limit = jnp.full((1, LANES), reach.astype(jnp.float32)) + 1.0
    return jnp.maximum(0.0, 1.0 - distance / limit)


def pairs_kernel(
    order, reach, zonal, own, control, up1, down1, up2, down2, prior, flow, seen, sea,
    to_up1, to_down1, to_up2, to_down2, to_up3, to_down3,
    sums, rows, own_b, control_b, up1_b, down1_b, up2_b, down2_b, sems, *, scale, zscale
):
    n = sums.shape[1]
    blocks = own.shape[0]
    always = [(own, own_b), (control, control_b)]
    near = [(up1, up1_b), (down1, down1_b)]
    far = [(up2, up2_b), (down2, down2_b)]

    def copies(i):
        found = {0: [], 1: [], 2: []}
        for k, (source, buffer) in enumerate(always + near + far):
            if i < source.shape[0]:
                at = order[i] if source is control else i
                copy = pltpu.make_async_copy(source.at[at], buffer.at[i], sems.at[k, i])
                found[k // 2].append(copy)
        return found

    for i in range(blocks):
        found = copies(i)
        for least in (0, 1, 2):
            if found[least]:

                @pl.when(reach[order[i]] >= least)
                def _(group=found[least]):
                    for copy in group:
                        copy.start()

    sums[...] = jnp.zeros(sums.shape, sums.dtype)
    levels, tall = zonal.shape[1:]
    for row in range(n):
        value = zonal[row // (levels * tall), row // tall % levels, row % tall]
        rows[row : row + 1] = jnp.full((1, LANES), value)

    for i in range(blocks):
        here = reach[order[i]]
        found = copies(i)

        def added(buffer, i=i):
            total = None
            for m in range(control.shape[1]):
                term = buffer[i, m].astype(jnp.float32) * control_b[i, m].astype(jnp.float32)
                total = term if total is None else total + term
            return total

        for copy in found[0]:
            copy.wait()
        sums[2] += weight_of(here, 0.0) * added(own_b)
        for least, up, down in ((1, up1_b, down1_b), (2, up2_b, down2_b)):
            if found[least]:

                @pl.when(here >= least)
                def _(least=least, up=up, down=down, here=here, group=found[least], added=added):
                    for copy in group:
                        copy.wait()
                    w = weight_of(here, float(least))
                    sums[2 + least] += w * added(up)
                    sums[2 - least] += w * added(down)

    part = [sums[o] * scale for o in range(5)]
    part[2] = part[2] + prior[...] * rows[...] * zscale
    for k in range(3):
        to_up1[k * n : (k + 1) * n] = part[2 + k]
        to_down1[k * n : (k + 1) * n] = part[k]
    for k in range(2):
        to_up2[k * n : (k + 1) * n] = part[3 + k]
        to_down2[k * n : (k + 1) * n] = part[k]
    to_up3[...] = part[4]
    to_down3[...] = part[0]
    for out in (to_up1, to_down1):
        at = 3 * n
        for source in (flow, seen):
            out[at : at + source.shape[0]] = source[...]
            at += source.shape[0]
        out[at : at + sea.shape[0]] = sea[...].astype(jnp.float32)


def mixed_kernel(
    rank, reach, down2_s, down1_s, own_s, up1_s, up2_s, own, up1, down1, up2, down2,
    out, own_b, up1_b, down1_b, up2_b, down2_b, out_b, sems, *, scale
):
    blocks = own.shape[0]
    pieces = [
        [(own, own_b, own_s)],
        [(up1, up1_b, up1_s), (down1, down1_b, down1_s)],
        [(up2, up2_b, up2_s), (down2, down2_b, down2_s)],
    ]

    def copies(j, d):
        found = []
        for k, (source, buffer, _) in enumerate(pieces[d]):
            at = j if d == 0 else jnp.minimum(rank[j], source.shape[0] - 1)
            sem = sems.at[max(0, 2 * d - 1) + k, j]
            found.append(pltpu.make_async_copy(source.at[at], buffer.at[j], sem))
        return found

    def written(j):
        return pltpu.make_async_copy(out_b.at[j], out.at[j], sems.at[5, j])

    for j in range(blocks):
        for d in range(REACH + 1):

            @pl.when(reach[j] >= d)
            def _(j=j, d=d):
                for copy in copies(j, d):
                    copy.start()

    def run(j, last):
        weights = [weight_of(reach[j], float(d)) for d in range(last + 1)]
        for d in range(last + 1):
            for copy in copies(j, d):
                copy.wait()
        scaled = [[sens[...] * scale for _, _, sens in pieces[d]] for d in range(last + 1)]
        for m in range(own.shape[1]):
            total = None
            for d in range(last + 1):
                near = None
                for (_, buffer, _), sens in zip(pieces[d], scaled[d]):
                    value = buffer[j, m].astype(jnp.float32) * sens
                    value = value.astype(jnp.bfloat16).astype(jnp.float32)
                    near = value if near is None else near + value
                near = weights[d] * near
                total = near if total is None else total + near
            out_b[j, m] = total

    def step(j, carry):
        for d in range(REACH + 1):
            here = reach[j]
            pl.when(here >= d if d == REACH else here == d)(lambda d=d: run(j, d))
        written(j).start()
        return carry

    lax.fori_loop(0, blocks, step, 0)
    for j in range(blocks):
        written(j).wait()


def lane(shape):
    return lax.broadcasted_iota(jnp.int32, shape, len(shape) - 1)


def gather_kernel(up, down, r1, m1, r2, m2, r3, m3, field, west_edge, east_edge):
    n = r3.shape[0]
    band = lax.axis_index("lat")
    low, high = band > 0, band < lax.axis_size("lat") - 1
    south = down[n : 2 * n] + r1[:n] + m1[:n] + r2[:n] + r3[...]
    mid = up[:n] + r1[n : 2 * n] + m1[n : 2 * n] + r2[n : 2 * n] + m2[:n]
    north = up[n : 2 * n] + r1[2 * n : 3 * n] + m1[2 * n : 3 * n] + m2[n : 2 * n] + m3[...]
    field[:, 12:PAD] = jnp.zeros((field.shape[0], PAD - 12, LANES), jnp.float32)
    south, north = jnp.where(low, south, 0.0), jnp.where(high, north, 0.0)
    for i in range(n // 4):
        field[i, 0:4] = south[4 * i : 4 * i + 4]
        field[i, 4:8] = mid[4 * i : 4 * i + 4]
        field[i, 8:12] = north[4 * i : 4 * i + 4]
    for i in range(n // 4, field.shape[0]):
        at = pl.ds(2 * n + 4 * i, 4)
        field[i, 0:4] = jnp.where(low, r1[at], 0.0)
        field[i, 4:8] = up[at]
        field[i, 8:12] = jnp.where(high, m1[at], 0.0)
    spot = lane((PAD, LANES)) // HALO
    for g in range(west_edge.shape[0]):
        west = jnp.zeros((PAD, LANES), jnp.float32)
        east = jnp.zeros((PAD, LANES), jnp.float32)
        for k in range(min(PACK, field.shape[0] - g * PACK)):
            value = field[g * PACK + k]
            at = HALO * k
            west = jnp.where(spot == k, pltpu.roll(value, at, 1) if at else value, west)
            east = jnp.where(spot == k, pltpu.roll(value, (at + HALO) % LANES, 1) if at + HALO < LANES else value, east)
        west_edge[g] = west
        east_edge[g] = east


def stencil_kernel(field, from_east, from_west, spread, out, zonal):
    n = out.shape[0] // 4
    cols = lane((PAD, LANES))

    def turn(value, amount):
        return pltpu.roll(value, amount % LANES, 1) if amount % LANES else value

    def wide(i):
        g, at = i // PACK, HALO * (i % PACK)
        right = turn(from_east[g], -at)
        left = turn(from_west[g], -at - HALO)
        beside = jnp.where(cols < HALO, right, jnp.where(cols >= LANES - HALO, left, 0.0))
        return field[i], beside

    def at_west(v):
        a, b = pltpu.roll(v[0], 1, 1), pltpu.roll(v[1], 1, 1)
        return jnp.where(cols == 0, b, a), jnp.where(cols == 0, a, b)

    def at_east(v):
        a, b = pltpu.roll(v[0], LANES - 1, 1), pltpu.roll(v[1], LANES - 1, 1)
        return jnp.where(cols == LANES - 1, b, a), jnp.where(cols == LANES - 1, a, b)

    def at_north(v):
        return tuple(pltpu.roll(x, PAD - 1, 0) for x in v)

    def at_south(v):
        return tuple(pltpu.roll(x, 1, 0) for x in v)

    def each(f, *vs):
        return tuple(f(*xs) for xs in zip(*vs))

    def mul(a, b):
        return each(lambda x, y: x * y, a, b)

    def sub(a, b):
        return each(lambda x, y: x - y, a, b)

    def total(*vs):
        return each(lambda *xs: sum(xs[1:], xs[0]), *vs)

    centre = 1.0 - 4.0 * NU
    levels = n // 3
    sea = wide(field.shape[0] - 1)
    for l in range(levels):
        cu, cv = wide(n + l), wide(n + levels + l)
        east_c = each(lambda x: NU - 0.5 * x, cu)
        west_c = each(lambda x: NU + 0.5 * x, cu)
        north_c = each(lambda x: NU - 0.5 * x, cv)
        south_c = each(lambda x: NU + 0.5 * x, cv)

        def tangent(f):
            return mul(
                sea,
                total(
                    each(lambda x: centre * x, f),
                    mul(east_c, at_east(f)),
                    mul(west_c, at_west(f)),
                    mul(north_c, at_north(f)),
                    mul(south_c, at_south(f)),
                ),
            )

        def adjoint(f):
            z = mul(sea, f)
            return total(
                each(lambda x: centre * x, z),
                at_west(mul(east_c, z)),
                at_east(mul(west_c, z)),
                at_south(mul(north_c, z)),
                at_north(mul(south_c, z)),
            )

        for t in range(3):
            i = t * levels + l
            first = tangent(wide(i))
            second = tangent(first)
            near = wide(n + 2 * levels + i)
            later = wide(n + 2 * levels + n + i)
            weighted = total(sub(first, near), adjoint(sub(second, later)))
            out[4 * i : 4 * i + 4] = adjoint(weighted)[0][4:8]
    zonal[...] = lax.dot_general(
        jnp.ones((zonal.shape[0], LANES), jnp.float32),
        out[...] * spread[...],
        (((1,), (1,)), ((), ())),
        precision=lax.Precision.HIGHEST,
        preferred_element_type=jnp.float32,
    )


def whole():
    return pl.BlockSpec(memory_space=VMEM)


def local(
    ens_control, perturbations, zonal_control, spread, currents, sea_mask, observed, loc_reach
):
    bands = lax.axis_size("lat")
    slabs = lax.axis_size("lon")
    members, tracers, levels, rows, columns = ens_control.shape
    blocks = loc_reach.shape[0]
    group = members // blocks
    cells = tracers * levels * rows
    scale = 1.0 / math.sqrt(members - 1)
    zscale = 1.0 / math.sqrt(columns * slabs)
    own = perturbations.reshape(blocks, group, cells, columns)
    control = ens_control.reshape(blocks, group, cells, columns)
    most = blocks - 1
    place = pl.BlockSpec(memory_space=pl.ANY)
    small = pl.BlockSpec(memory_space=SMEM)
    sending, order, rank, case = pl.pallas_call(
        sort_kernel,
        in_specs=[small, place],
        out_specs=[place, small, small, small],
        out_shape=[
            jax.ShapeDtypeStruct(own.shape, own.dtype),
            jax.ShapeDtypeStruct((blocks,), jnp.int32),
            jax.ShapeDtypeStruct((blocks,), jnp.int32),
            jax.ShapeDtypeStruct((1,), jnp.int32),
        ],
        scratch_shapes=[
            pltpu.VMEM(own.shape, own.dtype),
            pltpu.SemaphoreType.DMA((2, blocks)),
        ],
        name="sort",
    )(loc_reach, own)

    inner_on = [(b, b + 1) for b in range(bands) if b % ROW != ROW - 1]
    inner_back = [(b, b - 1) for b in range(bands) if b % ROW]
    firsts, lasts = range(0, bands, ROW), range(ROW - 1, bands, ROW)
    ends = [(b, (b + 1) % bands) for b in lasts] + [(b, (b - 1) % bands) for b in firsts]
    turns = [(b, b - ROW + 1) for b in lasts] + [(b, b + ROW - 1) for b in firsts]
    hops = [(b, (b + ROW) % bands) for b in firsts] + [(b, (b - ROW) % bands) for b in lasts]

    def exchange(near, far):
        def run(block):
            relay = near // 2
            bent = lax.ppermute(block[near - relay : near], "lat", turns)
            direct = lax.ppermute(block[: near - relay], "lat", ends)
            inner_up = lax.ppermute(block[:near], "lat", inner_back)
            inner_down = lax.ppermute(block[:near], "lat", inner_on)
            far_up, far_down = shift(block[:far], "lat", -2), shift(block[:far], "lat", 2)
            relayed = lax.ppermute(bent, "lat", hops)
            return tuple(
                pl.pallas_call(
                    place_kernel,
                    in_specs=[whole()] * 6,
                    out_specs=[place] * 4,
                    out_shape=[jax.ShapeDtypeStruct((most,) + block.shape[1:], block.dtype)] * 4,
                    scratch_shapes=[pltpu.SemaphoreType.DMA((6, 2))],
                    name="place",
                )(*held(inner_up, inner_down, direct, relayed, far_up, far_down))
            )

        return run

    sizes = send_sizes(most)
    cases = [exchange(near, far) for near in sizes for far in sizes[near]]
    up1, down1, up2, down2 = lax.optimization_barrier(lax.switch(case[0], cases, sending))

    items = tracers * levels
    lines = [x.reshape(-1, columns) for x in (spread, currents, observed, sea_mask)]
    beside = sum(x.shape[0] for x in lines[1:])
    messages = [3 * cells + beside] * 2 + [2 * cells] * 2 + [cells] * 2

    def buffers(*counts):
        return [pltpu.VMEM((n, group, cells, columns), own.dtype) for n in counts]

    to_up1, to_down1, to_up2, to_down2, to_up3, to_down3 = pl.pallas_call(
        functools.partial(pairs_kernel, scale=scale, zscale=zscale),
        in_specs=[small] * 3 + [place] * 6 + [whole()] * 4,
        out_specs=[whole()] * 6,
        scratch_shapes=[
            pltpu.VMEM((5, cells, columns), jnp.float32),
            pltpu.VMEM((cells, columns), jnp.float32),
            *buffers(blocks, blocks, most, most, most, most),
            pltpu.SemaphoreType.DMA((6, blocks)),
        ],
        out_shape=[pltpu.VMEM((n, columns), jnp.float32) for n in messages],
        name="pairs",
    )(order, loc_reach, zonal_control, sending, control, up1, down1, up2, down2, *lines)

    r1, m1 = shift(to_up1, "lat", 1), shift(to_down1, "lat", -1)
    r2, m2 = shift(to_up2, "lat", 2), shift(to_down2, "lat", -2)
    r3, m3 = shift(to_up3, "lat", 3), shift(to_down3, "lat", -3)
    total = items + beside // rows
    packs = -(-total // PACK)
    field, west_edge, east_edge = pl.pallas_call(
        gather_kernel,
        in_specs=[whole()] * 8,
        out_specs=[whole()] * 3,
        out_shape=[
            pltpu.VMEM((total, PAD, columns), jnp.float32),
            pltpu.VMEM((packs, PAD, columns), jnp.float32),
            pltpu.VMEM((packs, PAD, columns), jnp.float32),
        ],
        name="gather",
    )(*held(to_up1, to_down1, r1, m1, r2, m2, r3, m3))
    from_east = shift(west_edge, "lon", -1)
    from_west = shift(east_edge, "lon", 1)
    sensitivity, zonal_part = pl.pallas_call(
        stencil_kernel,
        in_specs=[whole()] * 4,
        out_specs=[whole()] * 2,
        out_shape=[
            pltpu.VMEM((cells, columns), jnp.float32),
            jax.ShapeDtypeStruct((slabs, cells), jnp.float32),
        ],
        name="stencil",
    )(*held(field, from_east, from_west), lines[0])

    everyone = lax.all_to_all(zonal_part, "lon", 0, 0, tiled=True)
    summed = jnp.sum(everyone, axis=0).reshape(zonal_control.shape)
    zonal_grad = zonal_control + summed * zscale

    sens = [shift(sensitivity, "lat", d) if d else sensitivity for d in (2, 1, 0, -1, -2)]
    grad = pl.pallas_call(
        functools.partial(mixed_kernel, scale=scale),
        in_specs=[small] * 2 + [whole()] * 5 + [place] * 5,
        out_specs=place,
        scratch_shapes=[
            *buffers(*[blocks] * 5),
            pltpu.VMEM((blocks, group, cells, columns), jnp.float32),
            pltpu.SemaphoreType.DMA((6, blocks)),
        ],
        out_shape=jax.ShapeDtypeStruct((blocks, group, cells, columns), jnp.float32),
        name="mixed",
    )(rank, loc_reach, *held(*sens), own, up1, down1, up2, down2)
    return grad.reshape(ens_control.shape), zonal_grad


def solution(mesh):
    return jax.shard_map(
        local,
        mesh=mesh,
        in_specs=(
            P(None, None, None, "lat", "lon"),
            P(None, None, None, "lat", "lon"),
            P(None, None, "lat"),
            P(None, None, "lat", "lon"),
            P(None, None, "lat", "lon"),
            P("lat", "lon"),
            P(None, None, None, "lat", "lon"),
            P(),
        ),
        out_specs=(P(None, None, None, "lat", "lon"), P(None, None, "lat")),
        check_vma=False,
    )
```

```python
import functools
import math

import jax
import jax.numpy as jnp
from jax import lax
from jax.experimental import pallas as pl
from jax.experimental.pallas import tpu as pltpu
from jax.sharding import PartitionSpec as P


NU = 0.2
REACH = 2
HALO = 4
PAD = 16
LANES = 128
PACK = LANES // HALO
LEAST = 3
FEW = 4
VMEM = pltpu.MemorySpace.VMEM
SMEM = pltpu.MemorySpace.SMEM


def shift(value, axis, distance):
    peers = lax.axis_size(axis)
    return lax.ppermute(value, axis, [((i - distance) % peers, i) for i in range(peers)])


def sort_kernel(reach, own, out, order, rank, case, sems):
    blocks = own.shape[0]
    for j in range(blocks):
        place = jnp.int32(0)
        for i in range(blocks):
            if i != j:
                ahead = reach[i] >= reach[j] if i < j else reach[i] > reach[j]
                place = place + ahead.astype(jnp.int32)
        rank[j] = place
        order[place] = j
        pltpu.make_async_copy(own.at[j], out.at[place], sems.at[j]).start()
    near, far = jnp.int32(0), jnp.int32(0)
    for j in range(blocks):
        near = near + (reach[j] >= 1).astype(jnp.int32)
        far = far + (reach[j] >= 2).astype(jnp.int32)
    near = jnp.maximum(near, LEAST)
    chosen = jnp.clip(far - 2, 0, FEW - 1)
    for n, first in enumerate(send_sizes(blocks - 1)[1]):
        chosen = chosen + jnp.where(near == LEAST + n, first, 0)
    case[0] = chosen
    for j in range(blocks):
        pltpu.make_async_copy(own.at[j], out.at[rank[j]], sems.at[j]).wait()


def held(*arrays):
    return [pltpu.with_memory_space_constraint(x, VMEM) for x in arrays]


def send_sizes(most):
    sizes, starts = [], []
    for near in range(LEAST, most + 1):
        starts.append(len(sizes))
        far = list(range(2, min(near, FEW) + 1))
        sizes += [(near, n) for n in far + [near] * (near > FEW)]
    return sizes, starts


def weight_of(reach, distance):
    limit = jnp.full((1, LANES), reach.astype(jnp.float32)) + 1.0
    return jnp.maximum(0.0, 1.0 - distance / limit)


def pairs_kernel(
    order, reach, zonal, own, control, up1, down1, up2, down2, prior, flow, seen, sea,
    to_up1, to_down1, to_up2, to_down2, to_up3, to_down3,
    sums, rows, own_b, control_b, up1_b, down1_b, up2_b, down2_b, sems, *, scale, zscale
):
    n = sums.shape[1]
    blocks = own.shape[0]
    always = [(own, own_b), (control, control_b)]
    near = [(up1, up1_b), (down1, down1_b)]
    far = [(up2, up2_b), (down2, down2_b)]

    def copies(i):
        found = {0: [], 1: [], 2: []}
        for k, (source, buffer) in enumerate(always + near + far):
            if i < source.shape[0]:
                at = order[i] if source is control else i
                copy = pltpu.make_async_copy(source.at[at], buffer.at[i], sems.at[k, i])
                found[k // 2].append(copy)
        return found

    for i in range(blocks):
        found = copies(i)
        for least in (0, 1, 2):
            if found[least]:

                @pl.when(reach[order[i]] >= least)
                def _(group=found[least]):
                    for copy in group:
                        copy.start()

    sums[...] = jnp.zeros(sums.shape, sums.dtype)
    levels, tall = zonal.shape[1:]
    for row in range(n):
        value = zonal[row // (levels * tall), row // tall % levels, row % tall]
        rows[row : row + 1] = jnp.full((1, LANES), value)

    for i in range(blocks):
        here = reach[order[i]]
        found = copies(i)

        def added(buffer, i=i):
            total = None
            for m in range(control.shape[1]):
                term = buffer[i, m].astype(jnp.float32) * control_b[i, m].astype(jnp.float32)
                total = term if total is None else total + term
            return total

        for copy in found[0]:
            copy.wait()
        sums[2] += weight_of(here, 0.0) * added(own_b)
        for least, up, down in ((1, up1_b, down1_b), (2, up2_b, down2_b)):
            if found[least]:

                @pl.when(here >= least)
                def _(least=least, up=up, down=down, here=here, group=found[least], added=added):
                    for copy in group:
                        copy.wait()
                    w = weight_of(here, float(least))
                    sums[2 + least] += w * added(up)
                    sums[2 - least] += w * added(down)

    part = [sums[o] * scale for o in range(5)]
    part[2] = part[2] + prior[...] * rows[...] * zscale
    for k in range(3):
        to_up1[k * n : (k + 1) * n] = part[2 + k]
        to_down1[k * n : (k + 1) * n] = part[k]
    for k in range(2):
        to_up2[k * n : (k + 1) * n] = part[3 + k]
        to_down2[k * n : (k + 1) * n] = part[k]
    to_up3[...] = part[4]
    to_down3[...] = part[0]
    for out in (to_up1, to_down1):
        at = 3 * n
        for source in (flow, seen):
            out[at : at + source.shape[0]] = source[...]
            at += source.shape[0]
        out[at : at + sea.shape[0]] = sea[...].astype(jnp.float32)


def mixed_kernel(
    rank, reach, down2_s, down1_s, own_s, up1_s, up2_s, own, up1, down1, up2, down2,
    out, own_b, up1_b, down1_b, up2_b, down2_b, out_b, sems, *, scale
):
    blocks = own.shape[0]
    pieces = [
        [(own, own_b, own_s)],
        [(up1, up1_b, up1_s), (down1, down1_b, down1_s)],
        [(up2, up2_b, up2_s), (down2, down2_b, down2_s)],
    ]

    def copies(j, d):
        found = []
        for k, (source, buffer, _) in enumerate(pieces[d]):
            at = j if d == 0 else jnp.minimum(rank[j], source.shape[0] - 1)
            sem = sems.at[max(0, 2 * d - 1) + k, j]
            found.append(pltpu.make_async_copy(source.at[at], buffer.at[j], sem))
        return found

    def written(j):
        return pltpu.make_async_copy(out_b.at[j], out.at[j], sems.at[5, j])

    for j in range(blocks):
        for d in range(REACH + 1):

            @pl.when(reach[j] >= d)
            def _(j=j, d=d):
                for copy in copies(j, d):
                    copy.start()

    def run(j, last):
        weights = [weight_of(reach[j], float(d)) for d in range(last + 1)]
        for d in range(last + 1):
            for copy in copies(j, d):
                copy.wait()
        scaled = [[sens[...] * scale for _, _, sens in pieces[d]] for d in range(last + 1)]
        for m in range(own.shape[1]):
            total = None
            for d in range(last + 1):
                near = None
                for (_, buffer, _), sens in zip(pieces[d], scaled[d]):
                    value = buffer[j, m].astype(jnp.float32) * sens
                    value = value.astype(jnp.bfloat16).astype(jnp.float32)
                    near = value if near is None else near + value
                near = weights[d] * near
                total = near if total is None else total + near
            out_b[j, m] = total

    def step(j, carry):
        for d in range(REACH + 1):
            here = reach[j]
            pl.when(here >= d if d == REACH else here == d)(lambda d=d: run(j, d))
        written(j).start()
        return carry

    lax.fori_loop(0, blocks, step, 0)
    for j in range(blocks):
        written(j).wait()


def lane(shape):
    return lax.broadcasted_iota(jnp.int32, shape, len(shape) - 1)


def gather_kernel(up, down, r1, m1, r2, m2, r3, m3, field, west_edge, east_edge):
    n = r3.shape[0]
    band = lax.axis_index("lat")
    low, high = band > 0, band < lax.axis_size("lat") - 1
    south = down[n : 2 * n] + r1[:n] + m1[:n] + r2[:n] + r3[...]
    mid = up[:n] + r1[n : 2 * n] + m1[n : 2 * n] + r2[n : 2 * n] + m2[:n]
    north = up[n : 2 * n] + r1[2 * n : 3 * n] + m1[2 * n : 3 * n] + m2[n : 2 * n] + m3[...]
    field[:, 12:PAD] = jnp.zeros((field.shape[0], PAD - 12, LANES), jnp.float32)
    south, north = jnp.where(low, south, 0.0), jnp.where(high, north, 0.0)
    for i in range(n // 4):
        field[i, 0:4] = south[4 * i : 4 * i + 4]
        field[i, 4:8] = mid[4 * i : 4 * i + 4]
        field[i, 8:12] = north[4 * i : 4 * i + 4]
    for i in range(n // 4, field.shape[0]):
        at = pl.ds(2 * n + 4 * i, 4)
        field[i, 0:4] = jnp.where(low, r1[at], 0.0)
        field[i, 4:8] = up[at]
        field[i, 8:12] = jnp.where(high, m1[at], 0.0)
    spot = lane((PAD, LANES)) // HALO
    for g in range(west_edge.shape[0]):
        west = jnp.zeros((PAD, LANES), jnp.float32)
        east = jnp.zeros((PAD, LANES), jnp.float32)
        for k in range(min(PACK, field.shape[0] - g * PACK)):
            value = field[g * PACK + k]
            at = HALO * k
            west = jnp.where(spot == k, pltpu.roll(value, at, 1) if at else value, west)
            east = jnp.where(spot == k, pltpu.roll(value, (at + HALO) % LANES, 1) if at + HALO < LANES else value, east)
        west_edge[g] = west
        east_edge[g] = east


def stencil_kernel(field, from_east, from_west, spread, out, zonal):
    n = out.shape[0] // 4
    cols = lane((PAD, LANES))

    def turn(value, amount):
        return pltpu.roll(value, amount % LANES, 1) if amount % LANES else value

    def wide(i):
        g, at = i // PACK, HALO * (i % PACK)
        right = turn(from_east[g], -at)
        left = turn(from_west[g], -at - HALO)
        beside = jnp.where(cols < HALO, right, jnp.where(cols >= LANES - HALO, left, 0.0))
        return field[i], beside

    def at_west(v):
        a, b = pltpu.roll(v[0], 1, 1), pltpu.roll(v[1], 1, 1)
        return jnp.where(cols == 0, b, a), jnp.where(cols == 0, a, b)

    def at_east(v):
        a, b = pltpu.roll(v[0], LANES - 1, 1), pltpu.roll(v[1], LANES - 1, 1)
        return jnp.where(cols == LANES - 1, b, a), jnp.where(cols == LANES - 1, a, b)

    def at_north(v):
        return tuple(pltpu.roll(x, PAD - 1, 0) for x in v)

    def at_south(v):
        return tuple(pltpu.roll(x, 1, 0) for x in v)

    def each(f, *vs):
        return tuple(f(*xs) for xs in zip(*vs))

    def mul(a, b):
        return each(lambda x, y: x * y, a, b)

    def sub(a, b):
        return each(lambda x, y: x - y, a, b)

    def total(*vs):
        return each(lambda *xs: sum(xs[1:], xs[0]), *vs)

    centre = 1.0 - 4.0 * NU
    levels = n // 3
    sea = wide(field.shape[0] - 1)
    for l in range(levels):
        cu, cv = wide(n + l), wide(n + levels + l)
        east_c = each(lambda x: NU - 0.5 * x, cu)
        west_c = each(lambda x: NU + 0.5 * x, cu)
        north_c = each(lambda x: NU - 0.5 * x, cv)
        south_c = each(lambda x: NU + 0.5 * x, cv)

        def tangent(f):
            return mul(
                sea,
                total(
                    each(lambda x: centre * x, f),
                    mul(east_c, at_east(f)),
                    mul(west_c, at_west(f)),
                    mul(north_c, at_north(f)),
                    mul(south_c, at_south(f)),
                ),
            )

        def adjoint(f):
            z = mul(sea, f)
            return total(
                each(lambda x: centre * x, z),
                at_west(mul(east_c, z)),
                at_east(mul(west_c, z)),
                at_south(mul(north_c, z)),
                at_north(mul(south_c, z)),
            )

        for t in range(3):
            i = t * levels + l
            first = tangent(wide(i))
            second = tangent(first)
            near = wide(n + 2 * levels + i)
            later = wide(n + 2 * levels + n + i)
            weighted = total(sub(first, near), adjoint(sub(second, later)))
            out[4 * i : 4 * i + 4] = adjoint(weighted)[0][4:8]
    zonal[...] = lax.dot_general(
        jnp.ones((zonal.shape[0], LANES), jnp.float32),
        out[...] * spread[...],
        (((1,), (1,)), ((), ())),
        precision=lax.Precision.HIGHEST,
        preferred_element_type=jnp.float32,
    )


def whole():
    return pl.BlockSpec(memory_space=VMEM)


def local(
    ens_control, perturbations, zonal_control, spread, currents, sea_mask, observed, loc_reach
):
    bands = lax.axis_size("lat")
    slabs = lax.axis_size("lon")
    members, tracers, levels, rows, columns = ens_control.shape
    blocks = loc_reach.shape[0]
    group = members // blocks
    cells = tracers * levels * rows
    scale = 1.0 / math.sqrt(members - 1)
    zscale = 1.0 / math.sqrt(columns * slabs)
    own = perturbations.reshape(blocks, group, cells, columns)
    control = ens_control.reshape(blocks, group, cells, columns)
    most = blocks - 1
    place = pl.BlockSpec(memory_space=pl.ANY)
    small = pl.BlockSpec(memory_space=SMEM)
    sending, order, rank, case = pl.pallas_call(
        sort_kernel,
        in_specs=[small, place],
        out_specs=[place, small, small, small],
        out_shape=[
            jax.ShapeDtypeStruct(own.shape, own.dtype),
            jax.ShapeDtypeStruct((blocks,), jnp.int32),
            jax.ShapeDtypeStruct((blocks,), jnp.int32),
            jax.ShapeDtypeStruct((1,), jnp.int32),
        ],
        scratch_shapes=[pltpu.SemaphoreType.DMA((blocks,))],
        name="sort",
    )(loc_reach, own)

    def exchange(near, far):
        def run(block):
            got = []
            for distance, n in ((-1, near), (1, near), (-2, far), (2, far)):
                moved = shift(block[:n], "lat", distance)
                rest = jnp.zeros((most - n,) + block.shape[1:], block.dtype)
                got.append(jnp.concatenate([moved, rest], axis=0) if n < most else moved)
            return tuple(got)

        return run

    cases = [exchange(near, far) for near, far in send_sizes(most)[0]]
    up1, down1, up2, down2 = lax.optimization_barrier(lax.switch(case[0], cases, sending))

    items = tracers * levels
    lines = [x.reshape(-1, columns) for x in (spread, currents, observed, sea_mask)]
    beside = sum(x.shape[0] for x in lines[1:])
    messages = [3 * cells + beside] * 2 + [2 * cells] * 2 + [cells] * 2

    def buffers(*counts):
        return [pltpu.VMEM((n, group, cells, columns), own.dtype) for n in counts]

    to_up1, to_down1, to_up2, to_down2, to_up3, to_down3 = pl.pallas_call(
        functools.partial(pairs_kernel, scale=scale, zscale=zscale),
        in_specs=[small] * 3 + [place] * 6 + [whole()] * 4,
        out_specs=[whole()] * 6,
        scratch_shapes=[
            pltpu.VMEM((5, cells, columns), jnp.float32),
            pltpu.VMEM((cells, columns), jnp.float32),
            *buffers(blocks, blocks, most, most, most, most),
            pltpu.SemaphoreType.DMA((6, blocks)),
        ],
        out_shape=[pltpu.VMEM((n, columns), jnp.float32) for n in messages],
        name="pairs",
    )(order, loc_reach, zonal_control, sending, control, up1, down1, up2, down2, *lines)

    r1, m1 = shift(to_up1, "lat", 1), shift(to_down1, "lat", -1)
    r2, m2 = shift(to_up2, "lat", 2), shift(to_down2, "lat", -2)
    r3, m3 = shift(to_up3, "lat", 3), shift(to_down3, "lat", -3)
    total = items + beside // rows
    packs = -(-total // PACK)
    field, west_edge, east_edge = pl.pallas_call(
        gather_kernel,
        in_specs=[whole()] * 8,
        out_specs=[whole()] * 3,
        out_shape=[
            pltpu.VMEM((total, PAD, columns), jnp.float32),
            pltpu.VMEM((packs, PAD, columns), jnp.float32),
            pltpu.VMEM((packs, PAD, columns), jnp.float32),
        ],
        name="gather",
    )(*held(to_up1, to_down1, r1, m1, r2, m2, r3, m3))
    from_east = shift(west_edge, "lon", -1)
    from_west = shift(east_edge, "lon", 1)
    sensitivity, zonal_part = pl.pallas_call(
        stencil_kernel,
        in_specs=[whole()] * 4,
        out_specs=[whole()] * 2,
        out_shape=[
            pltpu.VMEM((cells, columns), jnp.float32),
            jax.ShapeDtypeStruct((slabs, cells), jnp.float32),
        ],
        name="stencil",
    )(*held(field, from_east, from_west), lines[0])

    everyone = lax.all_to_all(zonal_part, "lon", 0, 0, tiled=True)
    summed = jnp.sum(everyone, axis=0).reshape(zonal_control.shape)
    zonal_grad = zonal_control + summed * zscale

    sens = [shift(sensitivity, "lat", d) if d else sensitivity for d in (2, 1, 0, -1, -2)]
    grad = pl.pallas_call(
        functools.partial(mixed_kernel, scale=scale),
        in_specs=[small] * 2 + [whole()] * 5 + [place] * 5,
        out_specs=place,
        scratch_shapes=[
            *buffers(*[blocks] * 5),
            pltpu.VMEM((blocks, group, cells, columns), jnp.float32),
            pltpu.SemaphoreType.DMA((6, blocks)),
        ],
        out_shape=jax.ShapeDtypeStruct((blocks, group, cells, columns), jnp.float32),
        name="mixed",
    )(rank, loc_reach, *held(*sens), own, up1, down1, up2, down2)
    return grad.reshape(ens_control.shape), zonal_grad


def solution(mesh):
    return jax.shard_map(
        local,
        mesh=mesh,
        in_specs=(
            P(None, None, None, "lat", "lon"),
            P(None, None, None, "lat", "lon"),
            P(None, None, "lat"),
            P(None, None, "lat", "lon"),
            P(None, None, "lat", "lon"),
            P("lat", "lon"),
            P(None, None, None, "lat", "lon"),
            P(),
        ),
        out_specs=(P(None, None, None, "lat", "lon"), P(None, None, "lat")),
        check_vma=False,
    )
```
